512 devices in a mesh: leaf: 64 (over y, z), samp: 8 (over x, core).
Axes of the slice: x: 4, y: 4, z: 16, core: 2. Of those that a mesh axis runs over, the one named last changes fastest.
Arguments:
- stiffness_block_row: bfloat16 [1024, 8, 128, 128], P('leaf'), may hold values from -2 to 2
- stored_block_column: int32 [1024, 8], P('leaf'), may hold values from 0 to 1023, as said below
- samples_t: bfloat16 [256, 131072], P('samp', 'leaf'), may hold values from -8 to 8
Outputs:
- products: float32 [256, 131072], P('samp', 'leaf')
- bases: float32 [256, 131072], P('samp', 'leaf')
- transfer_one: float32 [16384, 256], P('leaf', 'samp')
- transfer_two: float32 [16384, 256], P('leaf', 'samp')
- transfer_three: float32 [16384, 256], P('leaf', 'samp')
- top_factor: float32 [16384, 256], P('leaf', 'samp')
The draws below stay inside these ranges and needn't reach their ends.
Inputs may be any that keep to these rules, and one draw needn't show every extreme that they name: `stored_block_column`: slot 0 of block row r names block column r; the other slots name block columns of the same leaf, or of a neighbouring leaf within 4 block rows of the boundary that the two leaves share; the first block row of every leaf that has a neighbour on a side reaches exactly 4 block rows into it, and every one of those 4 block rows is named by some block row of the leaf.
All inputs are finite; a program needn't handle non-finite values.
Results may differ from the reference program's by a relative error of at most 0.0003.
Values may be sent and summed in bfloat16 or wider, within the bound.
A program may use at most 64 MiB of HBM per device.

```python
import math
import jax
import jax.numpy as jnp
from jax import lax

S = 256
BS = 128
NB = 8
HB = 4
LEVELS = 3
RDEV = 2048
N = 131072
BROWS = 1024
NODEROWS = 16384
N_LEAF = 64


def draw_stored_block_column(key, part):
    per_leaf = RDEV // BS
    leaf_total = BROWS // per_leaf
    row_index = jnp.arange(BROWS, dtype=jnp.int32)
    leaf_number = (row_index // per_leaf)[:, None]
    leaf_start = leaf_number * per_leaf
    row_in_leaf = (row_index % per_leaf)[:, None]
    key_own = jax.random.fold_in(key, 11)
    key_below = jax.random.fold_in(key, 23)
    key_above = jax.random.fold_in(key, 37)
    own_cols = leaf_start + jax.random.randint(key_own, (BROWS, 5), 0, per_leaf, dtype=jnp.int32)
    below_cols = leaf_start - HB + jax.random.randint(key_below, (BROWS, 2), 0, HB, dtype=jnp.int32)
    above_cols = leaf_start + per_leaf + jax.random.randint(key_above, (BROWS, 2), 0, HB, dtype=jnp.int32)
    first_slot = (jnp.arange(2, dtype=jnp.int32) == 0)[None, :]
    below_cycle = leaf_start - HB + row_in_leaf % HB
    above_cycle = leaf_start + per_leaf + (row_in_leaf + HB - 1) % HB
    below_cols = jnp.where(first_slot, below_cycle, below_cols)
    above_cols = jnp.where(first_slot, above_cycle, above_cols)
    below_cols = jnp.where(leaf_number > 0, below_cols, own_cols[:, 3:5])
    above_cols = jnp.where(leaf_number < leaf_total - 1, above_cols, own_cols[:, 3:5])
    joined = jnp.concatenate([row_index[:, None], own_cols[:, 0:3], below_cols, above_cols], axis=1)
    return joined.astype(jnp.int32)


def draw_stiffness_block_row(key, part):
    key_noise = jax.random.fold_in(key, 101)
    spread = 0.5 / (NB * BS) ** 0.5
    noise = jax.random.normal(key_noise, (BROWS, NB, BS, BS), jnp.float32)
    diagonal = jnp.eye(BS, dtype=jnp.float32)[None, None, :, :] / NB ** 0.5
    return (noise * spread + diagonal).astype(jnp.bfloat16)


def draw_samples_t(key, part):
    key_noise = jax.random.fold_in(key, 201)
    values = jnp.clip(jax.random.normal(key_noise, (S, N), jnp.float32), -6.0, 6.0)
    return values.astype(jnp.bfloat16)


def setup_inputs(seed: int = 0) -> dict:
    streams_of = jax.random.split(jax.random.key(seed), 4)
    stiffness_block_row = draw_stiffness_block_row(jax.random.fold_in(streams_of[3], 71), 0)
    stored_block_column = draw_stored_block_column(jax.random.fold_in(streams_of[3], 71), 0)
    samples_t = draw_samples_t(jax.random.fold_in(streams_of[3], 71), 0)
    return dict(stiffness_block_row=stiffness_block_row, stored_block_column=stored_block_column, samples_t=samples_t)


def lower_solve(factor, right_side):
    return jax.scipy.linalg.solve_triangular(factor, right_side, lower=True)

def reference(stiffness_block_row, stored_block_column, samples_t):
    per_leaf = RDEV // BS
    sample_blocks = samples_t.reshape(S, BROWS, BS)

    def one_leaf(leaf_input_vectors):
        leaf_blocks, leaf_cols, leaf_number = leaf_input_vectors
        picked = jnp.take(sample_blocks, leaf_cols.reshape(-1), axis=1).reshape(S, per_leaf, NB, BS)
        inside = leaf_cols // per_leaf == leaf_number
        terms = jnp.einsum('rkij,srkj->srki', leaf_blocks.astype(jnp.float32), picked.astype(jnp.float32))
        whole_sum = lax.optimization_barrier(jnp.sum(terms, axis=2))
        remote_sum = lax.optimization_barrier(jnp.sum(jnp.where(inside[None, :, :, None], jnp.zeros_like(terms), terms), axis=2))
        return (whole_sum.reshape(S, RDEV), remote_sum.reshape(S, RDEV))
    whole_sum, distant_portion = lax.map(one_leaf, (stiffness_block_row.reshape(N_LEAF, per_leaf, NB, BS, BS), stored_block_column.reshape(N_LEAF, per_leaf, NB), jnp.arange(N_LEAF, dtype=jnp.int32)))
    products = jnp.transpose(whole_sum, (1, 0, 2)).reshape(S, N)
    gramian_product = jnp.einsum('fjd,fwd->fjw', distant_portion, distant_portion, precision=lax.Precision.HIGHEST)
    factor = jnp.linalg.cholesky(gramian_product)
    leaf_basis = jax.vmap(lower_solve)(factor, distant_portion) * math.sqrt(RDEV)
    bases = jnp.transpose(leaf_basis, (1, 0, 2)).reshape(S, N)
    results = []
    for height in range(LEVELS):
        pairs = gramian_product.reshape(-1, 2, S, S)
        parent = pairs[:, 0] + pairs[:, 1]
        parent_low = jnp.linalg.cholesky(parent)
        blocks = jax.vmap(lower_solve)(jnp.repeat(parent_low, 2, axis=0), factor)
        results.append(jnp.repeat(blocks, 2 ** height, axis=0).reshape(NODEROWS, S))
        gramian_product, factor = (parent, parent_low)
    top_factor = jnp.repeat(factor, 2 ** LEVELS, axis=0).reshape(NODEROWS, S) / math.sqrt(2 ** LEVELS * RDEV)
    return (products, bases, results[0], results[1], results[2], top_factor)
```

```python
import functools, math
import jax, jax.numpy as jnp
from jax import lax
from jax.experimental import pallas as pl
from jax.experimental.pallas import tpu as pltpu

from jax.sharding import PartitionSpec as P

HB = 4
LEVELS = 3


def with_halo(cells, sides, width):
    for axis, dim in sides:
        count = lax.axis_size(axis)
        ends = count - 1
        head = lax.slice_in_dim(cells, 0, width, axis=dim)
        tail = lax.slice_in_dim(cells, cells.shape[dim] - width, cells.shape[dim], axis=dim)
        cells = jnp.concatenate(
            [
                lax.ppermute(tail, axis, [(i, (i + 1) % count) for i in range(ends)]),
                cells,
                lax.ppermute(head, axis, [((i + 1) % count, i) for i in range(ends)]),
            ],
            axis=dim,
        )
    return cells


def from_partner(block, axis, bit):
    count = lax.axis_size(axis)
    route = []
    for low in range(count):
        high = low | 1 << bit
        if high != low and high < count:
            route += [(low, high), (high, low)]
    return lax.ppermute(block, axis, route)


HI = lax.Precision.HIGHEST
RS = 136

def dot_tn(a, b):
    return lax.dot_general(a, b, (((0,), (0,)), ((), ())), precision=HI, preferred_element_type=jnp.float32)

def dot_nt(a, b):
    return lax.dot_general(a, b, (((1,), (1,)), ((), ())), precision=HI, preferred_element_type=jnp.float32)

def dot_nn(a, b):
    return lax.dot_general(a, b, (((1,), (0,)), ((), ())), precision=HI, preferred_element_type=jnp.float32)

def lane(v, j):
    return jnp.broadcast_to(v[:, j:j + 1], v.shape)

def rows(i):
    return pl.ds(i, 8, stride=RS)

def panel8(x, y, r0):
    a = [[lane(x[p], r0 + q) if q >= p else None for q in range(8)] for p in range(8)]
    for p in range(8):
        r = lax.rsqrt(a[p][p])
        u = [a[p][q] * r if q > p else None for q in range(8)]
        x[p] = x[p] * r
        y[p] = y[p] * r
        for s in range(p + 1, 8):
            for q in range(s, 8):
                a[s][q] = a[s][q] - u[s] * u[q]
            x[s] = x[s] - u[s] * x[p]
            y[s] = y[s] - u[s] * y[p]
    return x, y

def factor(X, Y, nb, sp=32):
    for t in range(128 // sp):
        base = t * sp
        if t:
            for b in range(nb):
                lhs = X[b * RS:b * RS + base, base:base + sp]
                rhs = jnp.concatenate([X[b * RS:b * RS + base, :], Y[b * RS:b * RS + base, :], Y[(4 + b) * RS:(4 + b) * RS + base, :]], axis=1)
                up = dot_tn(lhs, rhs)
                now = X[b * RS + base:b * RS + base + sp, :] - up[:, :128]
                X[b * RS + base:b * RS + base + sp, :] = now
                X[(4 + b) * RS + base:(4 + b) * RS + base + sp, :] = now
                Y[b * RS + base:b * RS + base + sp, :] -= up[:, 128:256]
                Y[(4 + b) * RS + base:(4 + b) * RS + base + sp, :] -= up[:, 256:]
        xs = [X[rows(base + i), :] for i in range(sp)]
        ys = [Y[rows(base + i), :] for i in range(sp)]
        for g in range(sp // 8):
            lo = g * 8
            nx, ny = panel8(xs[lo:lo + 8], ys[lo:lo + 8], base + lo)
            for p in range(8):
                X[rows(base + lo + p), :] = nx[p]
                Y[rows(base + lo + p), :] = ny[p]
            for i in range(lo + 8, sp):
                for p in range(8):
                    m = lane(nx[p], base + i)
                    xs[i] = xs[i] - m * nx[p]
                    ys[i] = ys[i] - m * ny[p]

def cholesky_inverse(G, U, W, X, Y, nb):
    r = lax.broadcasted_iota(jnp.int32, (128, 128), 0)
    c = lax.broadcasted_iota(jnp.int32, (128, 128), 1)
    eye = (r == c).astype(jnp.float32)
    up = c >= r
    zero = jnp.zeros((128, 128), jnp.float32)
    at = lambda g: slice(g * RS, g * RS + 128)
    for b in range(nb):
        X[at(b), :] = G[b, :128, :128]
        X[at(4 + b), :] = G[b, :128, :128]
        Y[at(b), :] = G[b, :128, 128:]
        Y[at(4 + b), :] = eye
    factor(X, Y, nb)
    for b in range(nb):
        u12 = Y[at(b), :]
        w11 = Y[at(4 + b), :]
        U[b, :128, :128] = jnp.where(up, X[at(b), :], zero)
        U[b, :128, 128:] = u12
        U[b, 128:, :128] = zero
        W[b, :128, :128] = w11
        W[b, :128, 128:] = zero
        z = dot_tn(u12, jnp.concatenate([u12, w11], axis=1))
        s = G[b, 128:, 128:] - z[:, :128]
        X[at(b), :] = s
        X[at(4 + b), :] = s
        Y[at(b), :] = -z[:, 128:]
        Y[at(4 + b), :] = eye
    factor(X, Y, nb)
    for b in range(nb):
        U[b, 128:, 128:] = jnp.where(up, X[at(b), :], zero)
        W[b, 128:, :128] = Y[at(b), :]
        W[b, 128:, 128:] = Y[at(4 + b), :]

def pick_blocks(sample_blocks, positions, keep_mask):
    sample_count = sample_blocks.shape[0]
    picked = jnp.take(sample_blocks, positions.reshape(-1), axis=1)
    picked = picked.reshape((sample_count,) + positions.shape + (sample_blocks.shape[2],))
    return jnp.where(keep_mask[None, :, :, None], picked, jnp.zeros_like(picked))


def shards(stiffness_block_row, stored_block_column, samples_t):
    block_sequence = stiffness_block_row.shape[2]
    blocks_here = stored_block_column.shape[0]
    sample_count = samples_t.shape[0]
    row_count = samples_t.shape[1]
    leaf_position_index = lax.axis_index("leaf")
    sample_index = lax.axis_index("samp")
    local_cols = stored_block_column - leaf_position_index * blocks_here
    inside = (local_cols >= 0) & (local_cols < blocks_here)
    own_blocks = samples_t.reshape(sample_count, blocks_here, block_sequence)
    near_terms = pick_blocks(own_blocks, jnp.clip(local_cols, 0, blocks_here - 1), inside)
    nearfield_portion = jnp.einsum(
        "rkij,srkj->sri", stiffness_block_row, near_terms, preferred_element_type=jnp.float32
    )
    window = with_halo(samples_t, (("leaf", 1),), HB * block_sequence)
    window_blocks = window.reshape(sample_count, blocks_here + 2 * HB, block_sequence)
    far_terms = pick_blocks(
        window_blocks,
        jnp.clip(local_cols + HB, 0, blocks_here + 2 * HB - 1),
        jnp.logical_not(inside),
    )
    far_part = jnp.einsum(
        "rkij,srkj->sri", stiffness_block_row, far_terms, preferred_element_type=jnp.float32
    )
    distant_portion = far_part.reshape(sample_count, row_count)
    products = (nearfield_portion + far_part).reshape(sample_count, row_count)
    gathered = lax.all_gather(distant_portion, "samp", axis=0, tiled=True)
    gramian_product = jnp.einsum("sr,tr->st", gathered, gathered, precision=lax.Precision.HIGHEST)

    level_grams = [gramian_product]
    current = gramian_product
    for height in range(LEVELS):
        partner = from_partner(current, "leaf", height)
        current = current + partner
        level_grams.append(current)
    outs = finish(level_grams, gathered, sample_count)
    return (products,) + tuple(outs)


def finish_kernel(g0, g1, g2, g3, z, bases, one, two, three, top, G, U, W, X, Y):
    for k, g in enumerate((g0, g1, g2, g3)):
        G[k] = g[...]
    cholesky_inverse(G, U, W, X, Y, 4)
    count = bases.shape[0]
    mine = pl.ds(pl.multiple_of(lax.axis_index("samp") * count, count), count)
    bases[...] = dot_nn(W[0, mine, :], z[...]) * math.sqrt(z.shape[1])
    for k, out in enumerate((one, two, three)):
        out[...] = dot_nt(W[k + 1], U[k, mine, :])
    top[...] = jnp.transpose(U[3, mine, :]) * (1.0 / math.sqrt(2**LEVELS * z.shape[1]))


def finish(grams, gathered, count):
    order, width = gathered.shape
    f32 = jnp.float32
    return pl.pallas_call(
        finish_kernel,
        out_shape=[jax.ShapeDtypeStruct((count, width), f32)] + [jax.ShapeDtypeStruct((order, count), f32)] * 4,
        in_specs=[pl.BlockSpec(memory_space=pltpu.VMEM)] * 5,
        out_specs=[pl.BlockSpec(memory_space=pltpu.VMEM)] * 5,
        scratch_shapes=[pltpu.VMEM((4, order, order), f32)] * 3 + [pltpu.VMEM((8 * RS, 128), f32)] * 2,
    )(*grams, gathered)


def solution(mesh):
    return jax.shard_map(
        shards,
        mesh=mesh,
        in_specs=(P("leaf", None, None, None), P("leaf", None), P("samp", "leaf")),
        out_specs=(
            P("samp", "leaf"),
            P("samp", "leaf"),
            P("leaf", "samp"),
            P("leaf", "samp"),
            P("leaf", "samp"),
            P("leaf", "samp"),
        ),
        check_vma=False,
    )
```

```python
import functools, math
import jax, jax.numpy as jnp
from jax import lax
from jax.experimental import pallas as pl
from jax.experimental.pallas import tpu as pltpu

from jax.sharding import PartitionSpec as P

HB = 4
NB = 8
LEVELS = 3
HOPS = (4, 5, 3, 6, 2, 7, 1, 0)
MESH = pl.DeviceIdType.MESH
HI = lax.Precision.HIGHEST
RS = 136

def dot_tn(a, b):
    return lax.dot_general(a, b, (((0,), (0,)), ((), ())), precision=HI, preferred_element_type=jnp.float32)

def dot_nt(a, b):
    return lax.dot_general(a, b, (((1,), (1,)), ((), ())), precision=HI, preferred_element_type=jnp.float32)

def dot_nt_fast(a, b):
    return lax.dot_general(a, b, (((1,), (1,)), ((), ())), preferred_element_type=jnp.float32)

def dot_nn(a, b):
    return lax.dot_general(a, b, (((1,), (0,)), ((), ())), precision=HI, preferred_element_type=jnp.float32)

def lane(v, j):
    return jnp.broadcast_to(v[:, j:j + 1], v.shape)

def rows(i):
    return pl.ds(i, 8, stride=RS)

def panel8(x, y, r0):
    a = [[lane(x[p], r0 + q) if q >= p else None for q in range(8)] for p in range(8)]
    for p in range(8):
        r = lax.rsqrt(a[p][p])
        u = [a[p][q] * r if q > p else None for q in range(8)]
        x[p] = x[p] * r
        y[p] = y[p] * r
        for s in range(p + 1, 8):
            for q in range(s, 8):
                a[s][q] = a[s][q] - u[s] * u[q]
            x[s] = x[s] - u[s] * x[p]
            y[s] = y[s] - u[s] * y[p]
    return x, y

def factor(X, Y, nb, sp=32):
    for t in range(128 // sp):
        base = t * sp
        if t:
            for b in range(nb):
                lhs = X[b * RS:b * RS + base, base:base + sp]
                rhs = jnp.concatenate([X[b * RS:b * RS + base, :], Y[b * RS:b * RS + base, :], Y[(4 + b) * RS:(4 + b) * RS + base, :]], axis=1)
                up = dot_tn(lhs, rhs)
                now = X[b * RS + base:b * RS + base + sp, :] - up[:, :128]
                X[b * RS + base:b * RS + base + sp, :] = now
                X[(4 + b) * RS + base:(4 + b) * RS + base + sp, :] = now
                Y[b * RS + base:b * RS + base + sp, :] -= up[:, 128:256]
                Y[(4 + b) * RS + base:(4 + b) * RS + base + sp, :] -= up[:, 256:]
        xs = [X[rows(base + i), :] for i in range(sp)]
        ys = [Y[rows(base + i), :] for i in range(sp)]
        for g in range(sp // 8):
            lo = g * 8
            nx, ny = panel8(xs[lo:lo + 8], ys[lo:lo + 8], base + lo)
            for p in range(8):
                X[rows(base + lo + p), :] = nx[p]
                Y[rows(base + lo + p), :] = ny[p]
            for i in range(lo + 8, sp):
                for p in range(8):
                    m = lane(nx[p], base + i)
                    xs[i] = xs[i] - m * nx[p]
                    ys[i] = ys[i] - m * ny[p]

def cholesky_inverse(G, U, W, X, Y, nb):
    r = lax.broadcasted_iota(jnp.int32, (128, 128), 0)
    c = lax.broadcasted_iota(jnp.int32, (128, 128), 1)
    eye = (r == c).astype(jnp.float32)
    up = c >= r
    zero = jnp.zeros((128, 128), jnp.float32)
    at = lambda g: slice(g * RS, g * RS + 128)
    for b in range(nb):
        X[at(b), :] = G(b, 0)
        X[at(4 + b), :] = G(b, 0)
        Y[at(b), :] = G(b, 1)
        Y[at(4 + b), :] = eye
    factor(X, Y, nb)
    for b in range(nb):
        u12 = Y[at(b), :]
        w11 = Y[at(4 + b), :]
        U[b, :128, :128] = jnp.where(up, X[at(b), :], zero)
        U[b, :128, 128:] = u12
        U[b, 128:, :128] = zero
        W[b, :128, :128] = w11
        W[b, :128, 128:] = zero
        z = dot_tn(u12, jnp.concatenate([u12, w11], axis=1))
        s = G(b, 2) - z[:, :128]
        X[at(b), :] = s
        X[at(4 + b), :] = s
        Y[at(b), :] = -z[:, 128:]
        Y[at(4 + b), :] = eye
    factor(X, Y, nb)
    for b in range(nb):
        U[b, 128:, 128:] = jnp.where(up, X[at(b), :], zero)
        W[b, 128:, :128] = Y[at(b), :]
        W[b, 128:, 128:] = Y[at(4 + b), :]

def greet(barrier, there, sample):
    pl.semaphore_signal(barrier, inc=1, device_id=(there, sample), device_id_type=MESH)


def window_kernel(leaves, own, win, halo_send, halo_recv):
    leaf = lax.axis_index("leaf")
    me = lax.axis_index("samp")
    group = lax.axis_size("samp")
    count = own.shape[0]
    width = HB * 128
    barrier = pltpu.get_barrier_semaphore()
    for hop in HOPS:
        peer = lax.rem(me + hop, group)
        @pl.when(leaf > 0)
        def _():
            greet(barrier, leaf - 1, peer)
        @pl.when(leaf < leaves - 1)
        def _():
            greet(barrier, leaf + 1, peer)
    @pl.when(leaf == 0)
    def _():
        win[:, :width] = jnp.zeros((win.shape[0], width), win.dtype)
    @pl.when(leaf == leaves - 1)
    def _():
        win[:, width:] = jnp.zeros((win.shape[0], width), win.dtype)
    neighbours = jnp.minimum(leaf, 1) + jnp.minimum(leaves - 1 - leaf, 1)
    pl.semaphore_wait(barrier, group * neighbours)

    def halo(side, sample_from, sample_to, hop):
        start = (own.shape[1] - width) * (1 - side)
        at = pl.ds(pl.multiple_of(sample_from * count, count), count)
        return pltpu.make_async_remote_copy(
            src_ref=own.at[:, pl.ds(start, width)],
            dst_ref=win.at[at, pl.ds(side * width, width)],
            send_sem=halo_send.at[side, hop],
            recv_sem=halo_recv.at[side, sample_from],
            device_id=(leaf + 1 - 2 * side, sample_to),
            device_id_type=MESH,
        )

    for hop in HOPS:
        peer = lax.rem(me + hop, group)
        @pl.when(leaf < leaves - 1)
        def _():
            halo(0, me, peer, hop).start()
        @pl.when(leaf > 0)
        def _():
            halo(1, me, peer, hop).start()
    for hop in HOPS:
        peer = lax.rem(me + hop, group)
        @pl.when(leaf > 0)
        def _():
            halo(0, peer, me, hop).wait_recv()
        @pl.when(leaf < leaves - 1)
        def _():
            halo(1, peer, me, hop).wait_recv()
    for hop in HOPS:
        peer = lax.rem(me + hop, group)
        @pl.when(leaf < leaves - 1)
        def _():
            halo(0, me, peer, hop).wait_send()
        @pl.when(leaf > 0)
        def _():
            halo(1, me, peer, hop).wait_send()


def window(leaves, samples_t):
    count = samples_t.shape[0]
    group = 8
    vmem = pl.BlockSpec(memory_space=pltpu.VMEM)
    return pl.pallas_call(
        functools.partial(window_kernel, leaves),
        out_shape=jax.ShapeDtypeStruct((group * count, 2 * HB * 128), samples_t.dtype),
        in_specs=[vmem],
        out_specs=vmem,
        scratch_shapes=[pltpu.SemaphoreType.DMA((2, group))] * 2,
        compiler_params=pltpu.CompilerParams(collective_id=0, has_side_effects=True),
        cost_estimate=pl.CostEstimate(flops=0, bytes_accessed=1 << 20, transcendentals=0),
    )(samples_t)


def block_row(A, picks, r):
    blocks = [A[r, k] for k in range(NB)]
    return dot_nt_fast(jnp.concatenate(picks, axis=1), jnp.concatenate(blocks, axis=1))


def product_kernel(cols, A, own, win, z, products, gram):
    leaf = lax.axis_index("leaf")
    count = own.shape[0]
    depth = cols.shape[0]
    mine = pl.ds(pl.multiple_of(lax.axis_index("samp") * count, count), count)

    def one_row(r):
        far, near = [], []
        for k in range(NB):
            local = cols[r, k] - leaf * depth
            inside = (local >= 0) & (local < depth)
            place = jnp.clip(jnp.where(local < 0, local + HB, local - depth + HB), 0, 2 * HB - 1)
            pick = win[:, pl.ds(pl.multiple_of(place * 128, 128), 128)]
            far.append(jnp.where(inside, jnp.zeros_like(pick), pick))
            pick = own[:, pl.ds(pl.multiple_of(jnp.clip(local, 0, depth - 1) * 128, 128), 128)]
            near.append(jnp.where(inside, pick, jnp.zeros_like(pick)))
        both = [jnp.concatenate([f, n], axis=0) for f, n in zip(far, near)]
        out = block_row(A, both, r)
        return out[:-count], out[-count:]

    gram[...] = jnp.zeros_like(gram)

    def step(q, carry):
        parts = [one_row(2 * q + i) for i in range(2)]
        pair = jnp.concatenate([p[0] for p in parts], axis=1)
        here = pl.ds(pl.multiple_of(q * 256, 256), 256)
        z[:, here] = pair
        products[:, here] = jnp.concatenate([p[1] for p in parts], axis=1)
        upper = dot_nt(pair[:128], pair)
        gram[0] += upper[:, :128]
        gram[1] += upper[:, 128:]
        gram[2] += dot_nt(pair[128:], pair[128:])
        return carry

    lax.fori_loop(0, depth // 2, step, 0)
    products[...] += z[mine, :]


def product(stiffness_block_row, stored_block_column, samples_t, win):
    f32 = jnp.float32
    count, width = samples_t.shape
    vmem = pl.BlockSpec(memory_space=pltpu.VMEM)
    return pl.pallas_call(
        product_kernel,
        out_shape=[
            jax.ShapeDtypeStruct((win.shape[0], width), f32),
            jax.ShapeDtypeStruct((count, width), f32),
            jax.ShapeDtypeStruct((3, 128, 128), f32),
        ],
        in_specs=[pl.BlockSpec(memory_space=pltpu.SMEM), vmem, vmem, vmem],
        out_specs=[vmem] * 3,
        cost_estimate=pl.CostEstimate(flops=10**10, bytes_accessed=8 << 20, transcendentals=0),
    )(stored_block_column, stiffness_block_row, samples_t, win)


def levels_kernel(gram, levels, part, got, pair_send, pair_recv, all_send, all_recv):
    leaf = lax.axis_index("leaf")
    me = lax.axis_index("samp")
    group = lax.axis_size("samp")
    barrier = pltpu.get_barrier_semaphore()
    partners = [leaf + (1 << h) - 2 * (1 << h) * lax.rem(leaf // (1 << h), 2) for h in range(LEVELS)]
    for h in reversed(range(LEVELS)):
        greet(barrier, partners[h], me)
    for hop in HOPS[:-1]:
        greet(barrier, leaf, lax.rem(me + hop, group))
    slab = 128 // group
    rows_here = pl.ds(pl.multiple_of(me * slab, slab), slab)
    for j in range(3):
        part[0, j * slab:(j + 1) * slab, :] = gram[j, rows_here, :]
    pl.semaphore_wait(barrier, group - 1 + LEVELS)

    def trade(h):
        return pltpu.make_async_remote_copy(
            src_ref=part.at[h], dst_ref=got.at[h], send_sem=pair_send.at[h], recv_sem=pair_recv.at[h],
            device_id=(partners[h], me), device_id_type=MESH,
        )

    def share(h, sample_from, sample_to, hop):
        return pltpu.make_async_remote_copy(
            src_ref=part.at[h + 1], dst_ref=levels.at[h, sample_from],
            send_sem=all_send.at[h, hop], recv_sem=all_recv.at[h, sample_from],
            device_id=(leaf, sample_to), device_id_type=MESH,
        )

    trade(0).start()
    for h in range(LEVELS):
        trade(h).wait_recv()
        total = part[h] + got[h]
        part[h + 1] = total
        if h + 1 < LEVELS:
            trade(h + 1).start()
        for hop in HOPS[:-1]:
            share(h, me, lax.rem(me + hop, group), hop).start()
        levels[h, me] = total
    for h in range(LEVELS):
        for hop in HOPS[:-1]:
            share(h, lax.rem(me + hop, group), me, hop).wait_recv()
    for h in range(LEVELS):
        trade(h).wait_send()
        for hop in HOPS[:-1]:
            share(h, me, lax.rem(me + hop, group), hop).wait_send()


def exchange(gram):
    f32 = jnp.float32
    group = 8
    slab = 128 // group
    vmem = pl.BlockSpec(memory_space=pltpu.VMEM)
    return pl.pallas_call(
        levels_kernel,
        out_shape=jax.ShapeDtypeStruct((LEVELS, group, 3 * slab, 128), f32),
        in_specs=[vmem],
        out_specs=vmem,
        scratch_shapes=[
            pltpu.VMEM((LEVELS + 1, 3 * slab, 128), f32),
            pltpu.VMEM((LEVELS, 3 * slab, 128), f32),
            pltpu.SemaphoreType.DMA((LEVELS,)),
            pltpu.SemaphoreType.DMA((LEVELS,)),
            pltpu.SemaphoreType.DMA((LEVELS, group)),
            pltpu.SemaphoreType.DMA((LEVELS, group)),
        ],
        compiler_params=pltpu.CompilerParams(collective_id=1, has_side_effects=True),
        cost_estimate=pl.CostEstimate(flops=0, bytes_accessed=1 << 20, transcendentals=0),
    )(gram)


def finish_kernel(g0, lv, z, bases, one, two, three, top, U, W, X, Y):
    count, width = bases.shape
    slab = lv.shape[2] // 3
    def block(b, j):
        if b == 0:
            return g0[j]
        return jnp.concatenate([lv[b - 1, s, j * slab:(j + 1) * slab, :] for s in range(lv.shape[1])], axis=0)
    cholesky_inverse(block, U, W, X, Y, 4)
    mine = pl.ds(pl.multiple_of(lax.axis_index("samp") * count, count), count)
    bases[...] = dot_nn(W[0, mine, :], z[...]) * math.sqrt(width)
    for k, out in enumerate((one, two, three)):
        out[...] = dot_nt(W[k + 1], U[k, mine, :])
    top[...] = jnp.transpose(U[3, mine, :]) * (1.0 / math.sqrt(2**LEVELS * width))


def finish(gram, levels, z, count):
    order, width = z.shape
    f32 = jnp.float32
    vmem = pl.BlockSpec(memory_space=pltpu.VMEM)
    return pl.pallas_call(
        finish_kernel,
        out_shape=[jax.ShapeDtypeStruct((count, width), f32)] + [jax.ShapeDtypeStruct((order, count), f32)] * 4,
        in_specs=[vmem] * 3,
        out_specs=[vmem] * 5,
        scratch_shapes=[pltpu.VMEM((4, order, order), f32)] * 2 + [pltpu.VMEM((8 * RS, 128), f32)] * 2,
        cost_estimate=pl.CostEstimate(flops=10**10, bytes_accessed=4 << 20, transcendentals=0),
    )(gram, levels, z)


def shards(leaves, stiffness_block_row, stored_block_column, samples_t):
    win = window(leaves, samples_t)
    z, products, gram = product(stiffness_block_row, stored_block_column, samples_t, win)
    levels = exchange(gram)
    return (products,) + tuple(finish(gram, levels, z, samples_t.shape[0]))


def solution(mesh):
    return jax.shard_map(
        functools.partial(shards, mesh.shape["leaf"]),
        mesh=mesh,
        in_specs=(P("leaf", None, None, None), P("leaf", None), P("samp", "leaf")),
        out_specs=(
            P("samp", "leaf"),
            P("samp", "leaf"),
            P("leaf", "samp"),
            P("leaf", "samp"),
            P("leaf", "samp"),
            P("leaf", "samp"),
        ),
        check_vma=False,
    )
```

```python
import functools, math
import jax, jax.numpy as jnp
from jax import lax
from jax.experimental import pallas as pl
from jax.experimental.pallas import tpu as pltpu

from jax.sharding import PartitionSpec as P

HB = 4
NB = 8
LEVELS = 3
HOPS = (4, 5, 3, 6, 2, 7, 1, 0)
MESH = pl.DeviceIdType.MESH
HI = lax.Precision.HIGHEST
RS = 136

def dot_tn(a, b):
    return lax.dot_general(a, b, (((0,), (0,)), ((), ())), precision=HI, preferred_element_type=jnp.float32)

def dot_nt(a, b):
    return lax.dot_general(a, b, (((1,), (1,)), ((), ())), precision=HI, preferred_element_type=jnp.float32)

def dot_nt_fast(a, b):
    return lax.dot_general(a, b, (((1,), (1,)), ((), ())), preferred_element_type=jnp.float32)

def dot_nn(a, b):
    return lax.dot_general(a, b, (((1,), (0,)), ((), ())), precision=HI, preferred_element_type=jnp.float32)

def lane(v, j):
    return jnp.broadcast_to(v[:, j:j + 1], v.shape)

def rows(i):
    return pl.ds(i, 8, stride=RS)

def panel8(x, y, r0):
    a = [[lane(x[p], r0 + q) if q >= p else None for q in range(8)] for p in range(8)]
    for p in range(8):
        r = lax.rsqrt(a[p][p])
        u = [a[p][q] * r if q > p else None for q in range(8)]
        x[p] = x[p] * r
        y[p] = y[p] * r
        for s in range(p + 1, 8):
            for q in range(s, 8):
                a[s][q] = a[s][q] - u[s] * u[q]
            x[s] = x[s] - u[s] * x[p]
            y[s] = y[s] - u[s] * y[p]
    return x, y

def factor(X, Y, nb, sp=32):
    for t in range(128 // sp):
        base = t * sp
        if t:
            for b in range(nb):
                lhs = X[b * RS:b * RS + base, base:base + sp]
                rhs = jnp.concatenate([X[b * RS:b * RS + base, :], Y[b * RS:b * RS + base, :], Y[(4 + b) * RS:(4 + b) * RS + base, :]], axis=1)
                up = dot_tn(lhs, rhs)
                now = X[b * RS + base:b * RS + base + sp, :] - up[:, :128]
                X[b * RS + base:b * RS + base + sp, :] = now
                X[(4 + b) * RS + base:(4 + b) * RS + base + sp, :] = now
                Y[b * RS + base:b * RS + base + sp, :] -= up[:, 128:256]
                Y[(4 + b) * RS + base:(4 + b) * RS + base + sp, :] -= up[:, 256:]
        xs = [X[rows(base + i), :] for i in range(sp)]
        ys = [Y[rows(base + i), :] for i in range(sp)]
        for g in range(sp // 8):
            lo = g * 8
            nx, ny = panel8(xs[lo:lo + 8], ys[lo:lo + 8], base + lo)
            for p in range(8):
                X[rows(base + lo + p), :] = nx[p]
                Y[rows(base + lo + p), :] = ny[p]
            for i in range(lo + 8, sp):
                for p in range(8):
                    m = lane(nx[p], base + i)
                    xs[i] = xs[i] - m * nx[p]
                    ys[i] = ys[i] - m * ny[p]

def cholesky_inverse(G, U, W, X, Y, nb):
    r = lax.broadcasted_iota(jnp.int32, (128, 128), 0)
    c = lax.broadcasted_iota(jnp.int32, (128, 128), 1)
    eye = (r == c).astype(jnp.float32)
    up = c >= r
    zero = jnp.zeros((128, 128), jnp.float32)
    at = lambda g: slice(g * RS, g * RS + 128)
    for b in range(nb):
        X[at(b), :] = G(b, 0)
        X[at(4 + b), :] = G(b, 0)
        Y[at(b), :] = G(b, 1)
        Y[at(4 + b), :] = eye
    factor(X, Y, nb)
    for b in range(nb):
        u12 = Y[at(b), :]
        w11 = Y[at(4 + b), :]
        U[b, :128, :128] = jnp.where(up, X[at(b), :], zero)
        U[b, :128, 128:] = u12
        U[b, 128:, :128] = zero
        W[b, :128, :128] = w11
        W[b, :128, 128:] = zero
        z = dot_tn(u12, jnp.concatenate([u12, w11], axis=1))
        s = G(b, 2) - z[:, :128]
        X[at(b), :] = s
        X[at(4 + b), :] = s
        Y[at(b), :] = -z[:, 128:]
        Y[at(4 + b), :] = eye
    factor(X, Y, nb)
    for b in range(nb):
        U[b, 128:, 128:] = jnp.where(up, X[at(b), :], zero)
        W[b, 128:, :128] = Y[at(b), :]
        W[b, 128:, 128:] = Y[at(4 + b), :]

def greet(barrier, there, sample):
    pl.semaphore_signal(barrier, inc=1, device_id=(there, sample), device_id_type=MESH)


def window_kernel(leaves, own, win, halo_send, east_send, west_send, mate_send, recv):
    leaf = lax.axis_index("leaf")
    me = lax.axis_index("samp")
    group = lax.axis_size("samp")
    chips = group // 2
    chip, core = me // 2, lax.rem(me, 2)
    count = own.shape[0]
    width = HB * 128
    east = 2 * lax.rem(chip + 1, chips) + core
    west = 2 * lax.rem(chip + chips - 1, chips) + core
    mate = 2 * chip + 1 - core
    barrier = pltpu.get_barrier_semaphore()
    @pl.when(leaf > 0)
    def _():
        greet(barrier, leaf - 1, me)
    @pl.when(leaf < leaves - 1)
    def _():
        greet(barrier, leaf + 1, me)
    for peer in (east, west, mate):
        greet(barrier, leaf, peer)
    @pl.when(leaf == 0)
    def _():
        win[:, :width] = jnp.zeros((win.shape[0], width), win.dtype)
    @pl.when(leaf == leaves - 1)
    def _():
        win[:, width:] = jnp.zeros((win.shape[0], width), win.dtype)
    neighbours = jnp.minimum(leaf, 1) + jnp.minimum(leaves - 1 - leaf, 1)
    pl.semaphore_wait(barrier, 3 + neighbours)

    def place(side, sample):
        return win.at[pl.ds(pl.multiple_of(sample * count, count), count), pl.ds(side * width, width)]

    def send(source, side, sample, send_sem, slot, there, to):
        return pltpu.make_async_remote_copy(
            src_ref=source, dst_ref=place(side, sample), send_sem=send_sem, recv_sem=recv.at[side, slot[0], slot[1]],
            device_id=(there, to), device_id_type=MESH,
        )

    def halo(side):
        tail = own.at[:, pl.ds((own.shape[1] - width) * (1 - side), width)]
        return send(tail, side, me, halo_send.at[side], (0, 0), leaf + 1 - 2 * side, me)

    def origin(away):
        return 2 * lax.rem(chip + away, chips) + core

    def to_east(side, away):
        return send(place(side, origin(away)), side, origin(away), east_send.at[side, away // 3],
                    ((away + chips - 1) % chips, 0), leaf, east)

    def to_west(side, away):
        return send(place(side, origin(away)), side, origin(away), west_send.at[side, away],
                    (away + 1, 0), leaf, west)

    def to_mate(side, away):
        return send(place(side, origin(away)), side, origin(away), mate_send.at[side, away], (away, 1), leaf, mate)

    def arrived(side, away, other):
        sample = 2 * lax.rem(chip + away, chips) + (1 - core if other else core)
        send(place(side, sample), side, sample, mate_send.at[side, away], (away, other), leaf, mate).wait_recv()

    def if_side(side, do):
        @pl.when((leaf < leaves - 1) if side else (leaf > 0))
        def _():
            do()

    @pl.when(leaf < leaves - 1)
    def _():
        halo(0).start()
    @pl.when(leaf > 0)
    def _():
        halo(1).start()

    def own_rows(side):
        def do():
            arrived(side, 0, 0)
            to_east(side, 0).start()
            to_west(side, 0).start()
            to_mate(side, 0).start()
        return do

    def onward(side):
        def do():
            away = 1 if side else chips - 1
            arrived(side, away, 0)
            (to_west(1, 1) if side else to_east(0, chips - 1)).start()
            to_mate(side, away).start()
        return do

    def back(side, away):
        def do():
            arrived(side, away, 0)
            to_mate(side, away).start()
        return do

    for side in (0, 1):
        if_side(side, own_rows(side))
    for side in (0, 1):
        if_side(side, onward(side))
    for side in (0, 1):
        if_side(side, back(side, chips - 1 if side else 1))
    for side in (0, 1):
        if_side(side, back(side, 2))

    def rest(side):
        def do():
            for away in range(chips):
                arrived(side, away, 1)
            to_east(side, 0).wait_send()
            to_west(side, 0).wait_send()
            (to_west(1, 1) if side else to_east(0, chips - 1)).wait_send()
            for away in range(chips):
                to_mate(side, away).wait_send()
        return do

    for side in (0, 1):
        if_side(side, rest(side))
    @pl.when(leaf < leaves - 1)
    def _():
        halo(0).wait_send()
    @pl.when(leaf > 0)
    def _():
        halo(1).wait_send()


def window(leaves, samples_t):
    count = samples_t.shape[0]
    group = 8
    vmem = pl.BlockSpec(memory_space=pltpu.VMEM)
    return pl.pallas_call(
        functools.partial(window_kernel, leaves),
        out_shape=jax.ShapeDtypeStruct((group * count, 2 * HB * 128), samples_t.dtype),
        in_specs=[vmem],
        out_specs=vmem,
        scratch_shapes=[
            pltpu.SemaphoreType.DMA((2,)),
            pltpu.SemaphoreType.DMA((2, 2)),
            pltpu.SemaphoreType.DMA((2, 2)),
            pltpu.SemaphoreType.DMA((2, group // 2)),
            pltpu.SemaphoreType.DMA((2, group // 2, 2)),
        ],
        compiler_params=pltpu.CompilerParams(collective_id=0, has_side_effects=True),
        cost_estimate=pl.CostEstimate(flops=0, bytes_accessed=1 << 20, transcendentals=0),
    )(samples_t)


def block_row(A, picks, r):
    blocks = [A[r, k] for k in range(NB)]
    return dot_nt_fast(jnp.concatenate(picks, axis=1), jnp.concatenate(blocks, axis=1))


def product_kernel(cols, A, own, win, z, products, gram):
    leaf = lax.axis_index("leaf")
    count = own.shape[0]
    depth = cols.shape[1]
    mine = pl.ds(pl.multiple_of(lax.axis_index("samp") * count, count), count)

    def one_row(r):
        far, near = [], []
        for k in range(NB):
            local = cols[k, r] - leaf * depth
            inside = (local >= 0) & (local < depth)
            place = jnp.clip(jnp.where(local < 0, local + HB, local - depth + HB), 0, 2 * HB - 1)
            pick = win[:, pl.ds(pl.multiple_of(place * 128, 128), 128)]
            far.append(jnp.where(inside, jnp.zeros_like(pick), pick))
            pick = own[:, pl.ds(pl.multiple_of(jnp.clip(local, 0, depth - 1) * 128, 128), 128)]
            near.append(jnp.where(inside, pick, jnp.zeros_like(pick)))
        both = [jnp.concatenate([f, n], axis=0) for f, n in zip(far, near)]
        out = block_row(A, both, r)
        return out[:-count], out[-count:]

    gram[...] = jnp.zeros_like(gram)

    def step(q, carry):
        parts = [one_row(2 * q + i) for i in range(2)]
        pair = jnp.concatenate([p[0] for p in parts], axis=1)
        here = pl.ds(pl.multiple_of(q * 256, 256), 256)
        z[:, here] = pair
        products[:, here] = jnp.concatenate([p[1] for p in parts], axis=1)
        upper = dot_nt(pair[:128], pair)
        gram[0] += upper[:, :128]
        gram[1] += upper[:, 128:]
        gram[2] += dot_nt(pair[128:], pair[128:])
        return carry

    lax.fori_loop(0, depth // 2, step, 0)
    products[...] += z[mine, :]


def product(stiffness_block_row, stored_block_column, samples_t, win):
    f32 = jnp.float32
    count, width = samples_t.shape
    vmem = pl.BlockSpec(memory_space=pltpu.VMEM)
    return pl.pallas_call(
        product_kernel,
        out_shape=[
            jax.ShapeDtypeStruct((win.shape[0], width), f32),
            jax.ShapeDtypeStruct((count, width), f32),
            jax.ShapeDtypeStruct((3, 128, 128), f32),
        ],
        in_specs=[pl.BlockSpec(memory_space=pltpu.SMEM), vmem, vmem, vmem],
        out_specs=[vmem] * 3,
        cost_estimate=pl.CostEstimate(flops=10**10, bytes_accessed=8 << 20, transcendentals=0),
    )(jnp.transpose(stored_block_column), stiffness_block_row, samples_t, win)


def levels_kernel(gram, levels, part, got, pair_send, pair_recv, all_send, all_recv):
    leaf = lax.axis_index("leaf")
    me = lax.axis_index("samp")
    group = lax.axis_size("samp")
    barrier = pltpu.get_barrier_semaphore()
    partners = [leaf + (1 << h) - 2 * (1 << h) * lax.rem(leaf // (1 << h), 2) for h in range(LEVELS)]
    for h in reversed(range(LEVELS)):
        greet(barrier, partners[h], me)
    for hop in HOPS[:-1]:
        greet(barrier, leaf, lax.rem(me + hop, group))
    slab = 128 // group
    rows_here = pl.ds(pl.multiple_of(me * slab, slab), slab)
    for j in range(3):
        part[0, j * slab:(j + 1) * slab, :] = gram[j, rows_here, :]
    pl.semaphore_wait(barrier, group - 1 + LEVELS)

    def trade(h):
        return pltpu.make_async_remote_copy(
            src_ref=part.at[h], dst_ref=got.at[h], send_sem=pair_send.at[h], recv_sem=pair_recv.at[h],
            device_id=(partners[h], me), device_id_type=MESH,
        )

    def share(h, sample_from, sample_to, hop):
        return pltpu.make_async_remote_copy(
            src_ref=part.at[h + 1], dst_ref=levels.at[h, sample_from],
            send_sem=all_send.at[h, hop], recv_sem=all_recv.at[h, sample_from],
            device_id=(leaf, sample_to), device_id_type=MESH,
        )

    trade(0).start()
    for h in range(LEVELS):
        trade(h).wait_recv()
        total = part[h] + got[h]
        part[h + 1] = total
        if h + 1 < LEVELS:
            trade(h + 1).start()
        for hop in HOPS[:-1]:
            share(h, me, lax.rem(me + hop, group), hop).start()
        levels[h, me] = total
    for h in range(LEVELS):
        for hop in HOPS[:-1]:
            share(h, lax.rem(me + hop, group), me, hop).wait_recv()
    for h in range(LEVELS):
        trade(h).wait_send()
        for hop in HOPS[:-1]:
            share(h, me, lax.rem(me + hop, group), hop).wait_send()


def exchange(gram):
    f32 = jnp.float32
    group = 8
    slab = 128 // group
    vmem = pl.BlockSpec(memory_space=pltpu.VMEM)
    return pl.pallas_call(
        levels_kernel,
        out_shape=jax.ShapeDtypeStruct((LEVELS, group, 3 * slab, 128), f32),
        in_specs=[vmem],
        out_specs=vmem,
        scratch_shapes=[
            pltpu.VMEM((LEVELS + 1, 3 * slab, 128), f32),
            pltpu.VMEM((LEVELS, 3 * slab, 128), f32),
            pltpu.SemaphoreType.DMA((LEVELS,)),
            pltpu.SemaphoreType.DMA((LEVELS,)),
            pltpu.SemaphoreType.DMA((LEVELS, group)),
            pltpu.SemaphoreType.DMA((LEVELS, group)),
        ],
        compiler_params=pltpu.CompilerParams(collective_id=1, has_side_effects=True),
        cost_estimate=pl.CostEstimate(flops=0, bytes_accessed=1 << 20, transcendentals=0),
    )(gram)


def finish_kernel(g0, lv, z, bases, one, two, three, top, U, W, X, Y):
    count, width = bases.shape
    slab = lv.shape[2] // 3
    def block(b, j):
        if b == 0:
            return g0[j]
        return jnp.concatenate([lv[b - 1, s, j * slab:(j + 1) * slab, :] for s in range(lv.shape[1])], axis=0)
    cholesky_inverse(block, U, W, X, Y, 4)
    mine = pl.ds(pl.multiple_of(lax.axis_index("samp") * count, count), count)
    bases[...] = dot_nn(W[0, mine, :], z[...]) * math.sqrt(width)
    for k, out in enumerate((one, two, three)):
        out[...] = dot_nt(U[k, mine, :], W[k + 1])
    top[...] = U[3, mine, :] * (1.0 / math.sqrt(2**LEVELS * width))


def finish(gram, levels, z, count):
    order, width = z.shape
    f32 = jnp.float32
    vmem = pl.BlockSpec(memory_space=pltpu.VMEM)
    return pl.pallas_call(
        finish_kernel,
        out_shape=[jax.ShapeDtypeStruct((count, width), f32)] + [jax.ShapeDtypeStruct((count, order), f32)] * 4,
        in_specs=[vmem] * 3,
        out_specs=[vmem] * 5,
        scratch_shapes=[pltpu.VMEM((4, order, order), f32)] * 2 + [pltpu.VMEM((8 * RS, 128), f32)] * 2,
        cost_estimate=pl.CostEstimate(flops=10**10, bytes_accessed=4 << 20, transcendentals=0),
    )(gram, levels, z)


def shards(leaves, stiffness_block_row, stored_block_column, samples_t):
    win = window(leaves, samples_t)
    z, products, gram = product(stiffness_block_row, stored_block_column, samples_t, win)
    levels = exchange(gram)
    bases, *transposed = finish(gram, levels, z, samples_t.shape[0])
    return (products, bases) + tuple(jnp.transpose(t) for t in transposed)


def solution(mesh):
    return jax.shard_map(
        functools.partial(shards, mesh.shape["leaf"]),
        mesh=mesh,
        in_specs=(P("leaf", None, None, None), P("leaf", None), P("samp", "leaf")),
        out_specs=(
            P("samp", "leaf"),
            P("samp", "leaf"),
            P("leaf", "samp"),
            P("leaf", "samp"),
            P("leaf", "samp"),
            P("leaf", "samp"),
        ),
        check_vma=False,
    )
```

```python
import functools, math
import jax, jax.numpy as jnp
from jax import lax
from jax.experimental import pallas as pl
from jax.experimental.pallas import tpu as pltpu

from jax.sharding import PartitionSpec as P

HB = 4
NB = 8
LEVELS = 3
HOPS = (4, 5, 3, 6, 2, 7, 1, 0)
MESH = pl.DeviceIdType.MESH
HI = lax.Precision.HIGHEST
RS = 136

def dot_tn(a, b):
    return lax.dot_general(a, b, (((0,), (0,)), ((), ())), precision=HI, preferred_element_type=jnp.float32)

def dot_nt(a, b):
    return lax.dot_general(a, b, (((1,), (1,)), ((), ())), precision=HI, preferred_element_type=jnp.float32)

def dot_nt_fast(a, b):
    return lax.dot_general(a, b, (((1,), (1,)), ((), ())), preferred_element_type=jnp.float32)

def dot_nn(a, b):
    return lax.dot_general(a, b, (((1,), (0,)), ((), ())), precision=HI, preferred_element_type=jnp.float32)

def lane(v, j):
    return jnp.broadcast_to(v[:, j:j + 1], v.shape)

def rows(i):
    return pl.ds(i, 8, stride=RS)

def diagonal(xs, base, lo):
    return [[lane(xs[lo + p], base + lo + q) if q >= p else None for q in range(8)] for p in range(8)]

def factor(X, Y, nb, sp=16):
    column = lax.broadcasted_iota(jnp.int32, (1, 128), 1)
    for t in range(128 // sp):
        base = t * sp
        if t:
            solved = column < base
            for b in range(nb):
                lhs = X[b * RS:b * RS + base, base:base + sp]
                left = jnp.where(solved, Y[(4 + b) * RS:(4 + b) * RS + base, :], X[b * RS:b * RS + base, :])
                up = dot_tn(lhs, jnp.concatenate([left, Y[b * RS:b * RS + base, :]], axis=1))
                now = X[b * RS + base:b * RS + base + sp, :] - up[:, :128]
                X[b * RS + base:b * RS + base + sp, :] = now
                X[(4 + b) * RS + base:(4 + b) * RS + base + sp, :] = now
                Y[b * RS + base:b * RS + base + sp, :] -= up[:, 128:]
                Y[(4 + b) * RS + base:(4 + b) * RS + base + sp, :] -= jnp.where(solved, up[:, :128], 0.0)
        xs = [X[rows(base + i), :] for i in range(sp)]
        ys = [Y[rows(base + i), :] for i in range(sp)]
        a = diagonal(xs, base, 0)
        for lo in range(0, sp, 8):
            ahead = diagonal(xs, base, lo + 8) if lo + 8 < sp else None
            for p in range(8):
                r = lax.rsqrt(a[p][p])
                inv = r * r
                x = xs[lo + p] * r
                y = ys[lo + p] * r
                xs[lo + p], ys[lo + p] = x, y
                X[rows(base + lo + p), :] = x
                Y[rows(base + lo + p), :] = y
                for s in range(p + 1, 8):
                    u = a[p][s] * r
                    xs[lo + s] = xs[lo + s] - u * x
                    ys[lo + s] = ys[lo + s] - u * y
                    for q in range(s, 8):
                        a[s][q] = a[s][q] - (a[p][s] * a[p][q]) * inv
                if ahead is not None:
                    m = [lane(x, base + lo + 8 + j) for j in range(8)]
                    for s in range(8):
                        for q in range(s, 8):
                            ahead[s][q] = ahead[s][q] - m[s] * m[q]
                        xs[lo + 8 + s] = xs[lo + 8 + s] - m[s] * x
                        ys[lo + 8 + s] = ys[lo + 8 + s] - m[s] * y
            for i in range(lo + 16, sp):
                for p in range(8):
                    m = lane(xs[lo + p], base + i)
                    xs[i] = xs[i] - m * xs[lo + p]
                    ys[i] = ys[i] - m * ys[lo + p]
            a = ahead

def cholesky_inverse(G, U, W, X, Y, nb):
    r = lax.broadcasted_iota(jnp.int32, (128, 128), 0)
    c = lax.broadcasted_iota(jnp.int32, (128, 128), 1)
    eye = (r == c).astype(jnp.float32)
    up = c >= r
    zero = jnp.zeros((128, 128), jnp.float32)
    at = lambda g: slice(g * RS, g * RS + 128)
    for b in range(nb):
        X[at(b), :] = G(b, 0)
        X[at(4 + b), :] = G(b, 0)
        Y[at(b), :] = G(b, 1)
        Y[at(4 + b), :] = eye
    factor(X, Y, nb)
    for b in range(nb):
        u12 = Y[at(b), :]
        w11 = Y[at(4 + b), :]
        U[b, :128, :128] = jnp.where(up, X[at(b), :], zero)
        U[b, :128, 128:] = u12
        U[b, 128:, :128] = zero
        W[b, :128, :128] = w11
        W[b, :128, 128:] = zero
        z = dot_tn(u12, jnp.concatenate([u12, w11], axis=1))
        s = G(b, 2) - z[:, :128]
        X[at(b), :] = s
        X[at(4 + b), :] = s
        Y[at(b), :] = -z[:, 128:]
        Y[at(4 + b), :] = eye
    factor(X, Y, nb)
    for b in range(nb):
        U[b, 128:, 128:] = jnp.where(up, X[at(b), :], zero)
        W[b, 128:, :128] = Y[at(b), :]
        W[b, 128:, 128:] = Y[at(4 + b), :]

def greet(barrier, there, sample):
    pl.semaphore_signal(barrier, inc=1, device_id=(there, sample), device_id_type=MESH)


def window_kernel(leaves, own, win, halo_send, east_send, west_send, mate_send, recv):
    leaf = lax.axis_index("leaf")
    me = lax.axis_index("samp")
    group = lax.axis_size("samp")
    chips = group // 2
    chip, core = me // 2, lax.rem(me, 2)
    count = own.shape[0]
    width = HB * 128
    east = 2 * lax.rem(chip + 1, chips) + core
    west = 2 * lax.rem(chip + chips - 1, chips) + core
    mate = 2 * chip + 1 - core
    barrier = pltpu.get_barrier_semaphore()
    @pl.when(leaf > 0)
    def _():
        greet(barrier, leaf - 1, me)
    @pl.when(leaf < leaves - 1)
    def _():
        greet(barrier, leaf + 1, me)
    for peer in (east, west, mate):
        greet(barrier, leaf, peer)
    @pl.when(leaf == 0)
    def _():
        win[:, :width] = jnp.zeros((win.shape[0], width), win.dtype)
    @pl.when(leaf == leaves - 1)
    def _():
        win[:, width:] = jnp.zeros((win.shape[0], width), win.dtype)
    neighbours = jnp.minimum(leaf, 1) + jnp.minimum(leaves - 1 - leaf, 1)
    pl.semaphore_wait(barrier, 3 + neighbours)

    def place(side, sample):
        return win.at[pl.ds(pl.multiple_of(sample * count, count), count), pl.ds(side * width, width)]

    def send(source, side, sample, send_sem, slot, there, to):
        return pltpu.make_async_remote_copy(
            src_ref=source, dst_ref=place(side, sample), send_sem=send_sem, recv_sem=recv.at[side, slot[0], slot[1]],
            device_id=(there, to), device_id_type=MESH,
        )

    def halo(side):
        tail = own.at[:, pl.ds((own.shape[1] - width) * (1 - side), width)]
        return send(tail, side, me, halo_send.at[side], (0, 0), leaf + 1 - 2 * side, me)

    def origin(away):
        return 2 * lax.rem(chip + away, chips) + core

    def to_east(side, away):
        return send(place(side, origin(away)), side, origin(away), east_send.at[side, away // 3],
                    ((away + chips - 1) % chips, 0), leaf, east)

    def to_west(side, away):
        return send(place(side, origin(away)), side, origin(away), west_send.at[side, away],
                    (away + 1, 0), leaf, west)

    def to_mate(side, away):
        return send(place(side, origin(away)), side, origin(away), mate_send.at[side, away], (away, 1), leaf, mate)

    def arrived(side, away, other):
        sample = 2 * lax.rem(chip + away, chips) + (1 - core if other else core)
        send(place(side, sample), side, sample, mate_send.at[side, away], (away, other), leaf, mate).wait_recv()

    def if_side(side, do):
        @pl.when((leaf < leaves - 1) if side else (leaf > 0))
        def _():
            do()

    @pl.when(leaf < leaves - 1)
    def _():
        halo(0).start()
    @pl.when(leaf > 0)
    def _():
        halo(1).start()

    def own_rows(side):
        def do():
            arrived(side, 0, 0)
            to_east(side, 0).start()
            to_west(side, 0).start()
            to_mate(side, 0).start()
        return do

    def onward(side):
        def do():
            away = 1 if side else chips - 1
            arrived(side, away, 0)
            (to_west(1, 1) if side else to_east(0, chips - 1)).start()
            to_mate(side, away).start()
        return do

    def back(side, away):
        def do():
            arrived(side, away, 0)
            to_mate(side, away).start()
        return do

    for side in (0, 1):
        if_side(side, own_rows(side))
    for side in (0, 1):
        if_side(side, onward(side))
    for side in (0, 1):
        if_side(side, back(side, chips - 1 if side else 1))
    for side in (0, 1):
        if_side(side, back(side, 2))

    def rest(side):
        def do():
            for away in range(chips):
                arrived(side, away, 1)
            to_east(side, 0).wait_send()
            to_west(side, 0).wait_send()
            (to_west(1, 1) if side else to_east(0, chips - 1)).wait_send()
            for away in range(chips):
                to_mate(side, away).wait_send()
        return do

    for side in (0, 1):
        if_side(side, rest(side))
    @pl.when(leaf < leaves - 1)
    def _():
        halo(0).wait_send()
    @pl.when(leaf > 0)
    def _():
        halo(1).wait_send()


def window(leaves, samples_t):
    count = samples_t.shape[0]
    group = 8
    vmem = pl.BlockSpec(memory_space=pltpu.VMEM)
    return pl.pallas_call(
        functools.partial(window_kernel, leaves),
        out_shape=jax.ShapeDtypeStruct((group * count, 2 * HB * 128), samples_t.dtype),
        in_specs=[vmem],
        out_specs=vmem,
        scratch_shapes=[
            pltpu.SemaphoreType.DMA((2,)),
            pltpu.SemaphoreType.DMA((2, 2)),
            pltpu.SemaphoreType.DMA((2, 2)),
            pltpu.SemaphoreType.DMA((2, group // 2)),
            pltpu.SemaphoreType.DMA((2, group // 2, 2)),
        ],
        compiler_params=pltpu.CompilerParams(collective_id=0, has_side_effects=True),
        cost_estimate=pl.CostEstimate(flops=0, bytes_accessed=1 << 20, transcendentals=0),
    )(samples_t)


def block_row(A, picks, r):
    blocks = [A[r, k] for k in range(NB)]
    return dot_nt_fast(jnp.concatenate(picks, axis=1), jnp.concatenate(blocks, axis=1))


def split3(x):
    high = x.astype(jnp.bfloat16)
    rest = x - high.astype(jnp.float32)
    mid = rest.astype(jnp.bfloat16)
    low = (rest - mid.astype(jnp.float32)).astype(jnp.bfloat16)
    return high, mid, low


def product_kernel(cols, A, own, win, z, products, gram, acc):
    leaf = lax.axis_index("leaf")
    count = own.shape[0]
    depth = cols.shape[1]
    here = A.shape[0]
    q = pl.program_id(0)
    mine = pl.ds(pl.multiple_of(lax.axis_index("samp") * count, count), count)

    def one_row(i):
        far, near = [], []
        for k in range(NB):
            local = cols[k, q * here + i] - leaf * depth
            inside = (local >= 0) & (local < depth)
            place = jnp.clip(jnp.where(local < 0, local + HB, local - depth + HB), 0, 2 * HB - 1)
            pick = win[:, pl.ds(pl.multiple_of(place * 128, 128), 128)]
            far.append(jnp.where(inside, jnp.zeros_like(pick), pick))
            pick = own[:, pl.ds(pl.multiple_of(jnp.clip(local, 0, depth - 1) * 128, 128), 128)]
            near.append(jnp.where(inside, pick, jnp.zeros_like(pick)))
        both = [jnp.concatenate([f, n], axis=0) for f, n in zip(far, near)]
        out = block_row(A, both, i)
        return out[:-count], out[-count:]

    parts = [one_row(i) for i in range(here)]
    pair = jnp.concatenate([p[0] for p in parts], axis=1)
    z[...] = pair
    products[...] = jnp.concatenate([p[1] for p in parts], axis=1) + z[mine, :]
    high, mid, low = split3(pair)
    tops = dot_nt_fast(high, jnp.concatenate([high, mid, low], axis=0))
    even = tops[:, :256] + dot_nt_fast(mid, mid)
    odd = tops[:, 256:512] + tops[:, 512:]

    @pl.when(q == 0)
    def _():
        acc[0] = even
        acc[1] = odd

    @pl.when(q > 0)
    def _():
        acc[0] += even
        acc[1] += odd

    @pl.when(q == pl.num_programs(0) - 1)
    def _():
        g = acc[0] + (acc[1] + jnp.transpose(acc[1]))
        gram[0] = g[:128, :128]
        gram[1] = g[:128, 128:]
        gram[2] = g[128:, 128:]


def product(stiffness_block_row, stored_block_column, samples_t, win):
    f32 = jnp.float32
    count, width = samples_t.shape
    depth = stored_block_column.shape[0]
    here = 8
    whole = lambda shape: pl.BlockSpec(shape, lambda q: (0,) * len(shape), pipeline_mode=pl.Buffered(1))
    return pl.pallas_call(
        product_kernel,
        out_shape=[
            jax.ShapeDtypeStruct((win.shape[0], width), f32),
            jax.ShapeDtypeStruct((count, width), f32),
            jax.ShapeDtypeStruct((3, 128, 128), f32),
        ],
        grid=(depth // here,),
        in_specs=[
            pl.BlockSpec(memory_space=pltpu.SMEM),
            pl.BlockSpec((here,) + stiffness_block_row.shape[1:], lambda q: (q, 0, 0, 0)),
            whole(samples_t.shape),
            whole(win.shape),
        ],
        out_specs=[
            pl.BlockSpec((win.shape[0], here * 128), lambda q: (0, q)),
            pl.BlockSpec((count, here * 128), lambda q: (0, q)),
            pl.BlockSpec((3, 128, 128), lambda q: (0, 0, 0)),
        ],
        scratch_shapes=[pltpu.VMEM((2, 256, 256), f32)],
        cost_estimate=pl.CostEstimate(flops=10**10, bytes_accessed=8 << 20, transcendentals=0),
    )(jnp.transpose(stored_block_column), stiffness_block_row, samples_t, win)


def levels_kernel(gram, levels, part, got, pair_send, pair_recv, all_send, all_recv):
    leaf = lax.axis_index("leaf")
    me = lax.axis_index("samp")
    group = lax.axis_size("samp")
    barrier = pltpu.get_barrier_semaphore()
    partners = [leaf + (1 << h) - 2 * (1 << h) * lax.rem(leaf // (1 << h), 2) for h in range(LEVELS)]
    for h in reversed(range(LEVELS)):
        greet(barrier, partners[h], me)
    for hop in HOPS[:-1]:
        greet(barrier, leaf, lax.rem(me + hop, group))
    slab = 128 // group
    rows_here = pl.ds(pl.multiple_of(me * slab, slab), slab)
    for j in range(3):
        part[0, j * slab:(j + 1) * slab, :] = gram[j, rows_here, :]
    pl.semaphore_wait(barrier, group - 1 + LEVELS)

    def trade(h):
        return pltpu.make_async_remote_copy(
            src_ref=part.at[h], dst_ref=got.at[h], send_sem=pair_send.at[h], recv_sem=pair_recv.at[h],
            device_id=(partners[h], me), device_id_type=MESH,
        )

    def share(h, sample_from, sample_to, hop):
        return pltpu.make_async_remote_copy(
            src_ref=part.at[h + 1], dst_ref=levels.at[h, sample_from],
            send_sem=all_send.at[h, hop], recv_sem=all_recv.at[h, sample_from],
            device_id=(leaf, sample_to), device_id_type=MESH,
        )

    trade(0).start()
    for h in range(LEVELS):
        trade(h).wait_recv()
        total = part[h] + got[h]
        part[h + 1] = total
        if h + 1 < LEVELS:
            trade(h + 1).start()
        for hop in HOPS[:-1]:
            share(h, me, lax.rem(me + hop, group), hop).start()
        levels[h, me] = total
    for h in range(LEVELS):
        for hop in HOPS[:-1]:
            share(h, lax.rem(me + hop, group), me, hop).wait_recv()
    for h in range(LEVELS):
        trade(h).wait_send()
        for hop in HOPS[:-1]:
            share(h, me, lax.rem(me + hop, group), hop).wait_send()


def exchange(gram):
    f32 = jnp.float32
    group = 8
    slab = 128 // group
    vmem = pl.BlockSpec(memory_space=pltpu.VMEM)
    return pl.pallas_call(
        levels_kernel,
        out_shape=jax.ShapeDtypeStruct((LEVELS, group, 3 * slab, 128), f32),
        in_specs=[vmem],
        out_specs=vmem,
        scratch_shapes=[
            pltpu.VMEM((LEVELS + 1, 3 * slab, 128), f32),
            pltpu.VMEM((LEVELS, 3 * slab, 128), f32),
            pltpu.SemaphoreType.DMA((LEVELS,)),
            pltpu.SemaphoreType.DMA((LEVELS,)),
            pltpu.SemaphoreType.DMA((LEVELS, group)),
            pltpu.SemaphoreType.DMA((LEVELS, group)),
        ],
        compiler_params=pltpu.CompilerParams(collective_id=1, has_side_effects=True),
        cost_estimate=pl.CostEstimate(flops=0, bytes_accessed=1 << 20, transcendentals=0),
    )(gram)


def finish_kernel(g0, lv, z_far, bases, one, two, three, top, U, W, X, Y, z, z_sem):
    count, width = bases.shape
    load = pltpu.make_async_copy(z_far, z, z_sem)
    load.start()
    slab = lv.shape[2] // 3
    def block(b, j):
        if b == 0:
            return g0[j]
        return jnp.concatenate([lv[b - 1, s, j * slab:(j + 1) * slab, :] for s in range(lv.shape[1])], axis=0)
    cholesky_inverse(block, U, W, X, Y, 4)
    mine = pl.ds(pl.multiple_of(lax.axis_index("samp") * count, count), count)
    load.wait()
    bases[...] = dot_nn(W[0, mine, :], z[...]) * math.sqrt(width)
    for k, out in enumerate((one, two, three)):
        out[...] = dot_nt(U[k, mine, :], W[k + 1])
    top[...] = U[3, mine, :] * (1.0 / math.sqrt(2**LEVELS * width))


def finish(gram, levels, z, count):
    order, width = z.shape
    f32 = jnp.float32
    vmem = pl.BlockSpec(memory_space=pltpu.VMEM)
    return pl.pallas_call(
        finish_kernel,
        out_shape=[jax.ShapeDtypeStruct((count, width), f32)] + [jax.ShapeDtypeStruct((count, order), f32)] * 4,
        in_specs=[vmem, vmem, pl.BlockSpec(memory_space=pl.ANY)],
        out_specs=[vmem] * 5,
        scratch_shapes=[pltpu.VMEM((4, order, order), f32)] * 2 + [pltpu.VMEM((8 * RS, 128), f32)] * 2 + [pltpu.VMEM((order, width), f32), pltpu.SemaphoreType.DMA],
        cost_estimate=pl.CostEstimate(flops=10**10, bytes_accessed=4 << 20, transcendentals=0),
    )(gram, levels, z)


def shards(leaves, stiffness_block_row, stored_block_column, samples_t):
    win = window(leaves, samples_t)
    z, products, gram = product(stiffness_block_row, stored_block_column, samples_t, win)
    levels = exchange(gram)
    bases, *transposed = finish(gram, levels, z, samples_t.shape[0])
    return (products, bases) + tuple(jnp.transpose(t) for t in transposed)


def solution(mesh):
    return jax.shard_map(
        functools.partial(shards, mesh.shape["leaf"]),
        mesh=mesh,
        in_specs=(P("leaf", None, None, None), P("leaf", None), P("samp", "leaf")),
        out_specs=(
            P("samp", "leaf"),
            P("samp", "leaf"),
            P("leaf", "samp"),
            P("leaf", "samp"),
            P("leaf", "samp"),
            P("leaf", "samp"),
        ),
        check_vma=False,
    )
```

```python
import functools, math
import jax, jax.numpy as jnp
from jax import lax
from jax.experimental import pallas as pl
from jax.experimental.pallas import tpu as pltpu

from jax.sharding import PartitionSpec as P

HB = 4
NB = 8
LEVELS = 3
HOPS = (4, 5, 3, 6, 2, 7, 1, 0)
MESH = pl.DeviceIdType.MESH
HI = lax.Precision.HIGHEST
RS = 136

def dot_tn(a, b):
    return lax.dot_general(a, b, (((0,), (0,)), ((), ())), precision=HI, preferred_element_type=jnp.float32)

def dot_nt(a, b):
    return lax.dot_general(a, b, (((1,), (1,)), ((), ())), precision=HI, preferred_element_type=jnp.float32)

def dot_nt_fast(a, b):
    return lax.dot_general(a, b, (((1,), (1,)), ((), ())), preferred_element_type=jnp.float32)

def dot_nn(a, b):
    return lax.dot_general(a, b, (((1,), (0,)), ((), ())), precision=HI, preferred_element_type=jnp.float32)

def lane(v, j):
    return jnp.broadcast_to(v[:, j:j + 1], v.shape)

def rows(i):
    return pl.ds(i, 8, stride=RS)

def diagonal(xs, base, lo):
    return [[lane(xs[lo + p], base + lo + q) if q >= p else None for q in range(8)] for p in range(8)]

def factor(X, Y, nb, sp=16):
    column = lax.broadcasted_iota(jnp.int32, (1, 128), 1)
    for t in range(128 // sp):
        base = t * sp
        if t:
            solved = column < base
            for b in range(nb):
                lhs = X[b * RS:b * RS + base, base:base + sp]
                left = jnp.where(solved, Y[(4 + b) * RS:(4 + b) * RS + base, :], X[b * RS:b * RS + base, :])
                up = dot_tn(lhs, jnp.concatenate([left, Y[b * RS:b * RS + base, :]], axis=1))
                now = X[b * RS + base:b * RS + base + sp, :] - up[:, :128]
                X[b * RS + base:b * RS + base + sp, :] = now
                X[(4 + b) * RS + base:(4 + b) * RS + base + sp, :] = now
                Y[b * RS + base:b * RS + base + sp, :] -= up[:, 128:]
                Y[(4 + b) * RS + base:(4 + b) * RS + base + sp, :] -= jnp.where(solved, up[:, :128], 0.0)
        xs = [X[rows(base + i), :] for i in range(sp)]
        ys = [Y[rows(base + i), :] for i in range(sp)]
        a = diagonal(xs, base, 0)
        for lo in range(0, sp, 8):
            ahead = diagonal(xs, base, lo + 8) if lo + 8 < sp else None
            for p in range(8):
                r = lax.rsqrt(a[p][p])
                inv = r * r
                x = xs[lo + p] * r
                y = ys[lo + p] * r
                xs[lo + p], ys[lo + p] = x, y
                X[rows(base + lo + p), :] = x
                Y[rows(base + lo + p), :] = y
                for s in range(p + 1, 8):
                    u = a[p][s] * r
                    xs[lo + s] = xs[lo + s] - u * x
                    ys[lo + s] = ys[lo + s] - u * y
                    for q in range(s, 8):
                        a[s][q] = a[s][q] - (a[p][s] * a[p][q]) * inv
                if ahead is not None:
                    m = [lane(x, base + lo + 8 + j) for j in range(8)]
                    for s in range(8):
                        for q in range(s, 8):
                            ahead[s][q] = ahead[s][q] - m[s] * m[q]
                        xs[lo + 8 + s] = xs[lo + 8 + s] - m[s] * x
                        ys[lo + 8 + s] = ys[lo + 8 + s] - m[s] * y
            for i in range(lo + 16, sp):
                for p in range(8):
                    m = lane(xs[lo + p], base + i)
                    xs[i] = xs[i] - m * xs[lo + p]
                    ys[i] = ys[i] - m * ys[lo + p]
            a = ahead

def cholesky_inverse(G, U, W, X, Y, nb):
    r = lax.broadcasted_iota(jnp.int32, (128, 128), 0)
    c = lax.broadcasted_iota(jnp.int32, (128, 128), 1)
    eye = (r == c).astype(jnp.float32)
    up = c >= r
    zero = jnp.zeros((128, 128), jnp.float32)
    at = lambda g: slice(g * RS, g * RS + 128)
    for b in range(nb):
        X[at(b), :] = G(b, 0)
        X[at(4 + b), :] = G(b, 0)
        Y[at(b), :] = G(b, 1)
        Y[at(4 + b), :] = eye
    factor(X, Y, nb)
    for b in range(nb):
        u12 = Y[at(b), :]
        w11 = Y[at(4 + b), :]
        U[b, :128, :128] = jnp.where(up, X[at(b), :], zero)
        U[b, :128, 128:] = u12
        U[b, 128:, :128] = zero
        W[b, :128, :128] = w11
        W[b, :128, 128:] = zero
        z = dot_tn(u12, jnp.concatenate([u12, w11], axis=1))
        s = G(b, 2) - z[:, :128]
        X[at(b), :] = s
        X[at(4 + b), :] = s
        Y[at(b), :] = -z[:, 128:]
        Y[at(4 + b), :] = eye
    factor(X, Y, nb)
    for b in range(nb):
        U[b, 128:, 128:] = jnp.where(up, X[at(b), :], zero)
        W[b, 128:, :128] = Y[at(b), :]
        W[b, 128:, 128:] = Y[at(4 + b), :]

def greet(barrier, there, sample):
    pl.semaphore_signal(barrier, inc=1, device_id=(there, sample), device_id_type=MESH)


def split3(x):
    high = x.astype(jnp.bfloat16)
    rest = x - high.astype(jnp.float32)
    mid = rest.astype(jnp.bfloat16)
    low = (rest - mid.astype(jnp.float32)).astype(jnp.bfloat16)
    return high, mid, low


def gather_kernel(leaves, cols, stiff, own, z_out, near, gram, levels,
                  A, z, win, home, acc, part, got, load_sem, z_sem,
                  halo_send, east_send, west_send, mate_send, recv, pair_send, pair_recv, all_send, all_recv):
    load = pltpu.make_async_copy(stiff, A, load_sem)
    load.start()
    leaf = lax.axis_index("leaf")
    me = lax.axis_index("samp")
    group = lax.axis_size("samp")
    chips = group // 2
    chip, core = me // 2, lax.rem(me, 2)
    count = own.shape[0]
    width = HB * 128
    east = 2 * lax.rem(chip + 1, chips) + core
    west = 2 * lax.rem(chip + chips - 1, chips) + core
    mate = 2 * chip + 1 - core
    barrier = pltpu.get_barrier_semaphore()
    @pl.when(leaf > 0)
    def _():
        greet(barrier, leaf - 1, me)
    @pl.when(leaf < leaves - 1)
    def _():
        greet(barrier, leaf + 1, me)
    for hop in HOPS[:-1]:
        greet(barrier, leaf, lax.rem(me + hop, group))
    partners = [leaf + (1 << h) - 2 * (1 << h) * lax.rem(leaf // (1 << h), 2) for h in range(LEVELS)]
    for h in range(1, LEVELS):
        greet(barrier, partners[h], me)
    depth = own.shape[1] // 128
    win[HB:HB + depth] = jnp.zeros((depth,) + win.shape[1:], win.dtype)
    for edge in (0, HB + depth):
        home[edge:edge + HB] = jnp.zeros((HB,) + home.shape[1:], home.dtype)
    for j in range(depth):
        home[HB + j] = own[:, j * 128:(j + 1) * 128]
    @pl.when(leaf == 0)
    def _():
        win[:HB] = jnp.zeros((HB,) + win.shape[1:], win.dtype)
    @pl.when(leaf == leaves - 1)
    def _():
        win[HB + depth:] = jnp.zeros((HB,) + win.shape[1:], win.dtype)
    neighbours = jnp.minimum(leaf, 1) + jnp.minimum(leaves - 1 - leaf, 1)
    pl.semaphore_wait(barrier, group - 1 + LEVELS - 1 + neighbours)

    def place(side, sample):
        return win.at[pl.ds(side * (HB + depth), HB), pl.ds(pl.multiple_of(sample * count, count), count), :]

    def send(source, side, sample, send_sem, slot, there, to):
        return pltpu.make_async_remote_copy(
            src_ref=source, dst_ref=place(side, sample), send_sem=send_sem, recv_sem=recv.at[side, slot[0], slot[1]],
            device_id=(there, to), device_id_type=MESH,
        )

    def halo(side):
        first = HB + (depth - HB) * (1 - side)
        return send(home.at[pl.ds(first, HB)], side, me, halo_send.at[side], (0, 0), leaf + 1 - 2 * side, me)

    def origin(away):
        return 2 * lax.rem(chip + away, chips) + core

    def to_east(side, away):
        return send(place(side, origin(away)), side, origin(away), east_send.at[side, away // 3],
                    ((away + chips - 1) % chips, 0), leaf, east)

    def to_west(side, away):
        return send(place(side, origin(away)), side, origin(away), west_send.at[side, away],
                    (away + 1, 0), leaf, west)

    def to_mate(side, away):
        return send(place(side, origin(away)), side, origin(away), mate_send.at[side, away], (away, 1), leaf, mate)

    def arrived(side, away, other):
        sample = 2 * lax.rem(chip + away, chips) + (1 - core if other else core)
        send(place(side, sample), side, sample, mate_send.at[side, away], (away, other), leaf, mate).wait_recv()

    def if_side(side, do):
        @pl.when((leaf < leaves - 1) if side else (leaf > 0))
        def _():
            do()

    @pl.when(leaf < leaves - 1)
    def _():
        halo(0).start()
    @pl.when(leaf > 0)
    def _():
        halo(1).start()

    def own_rows(side):
        def do():
            arrived(side, 0, 0)
            to_east(side, 0).start()
            to_west(side, 0).start()
            to_mate(side, 0).start()
        return do

    def onward(side):
        def do():
            away = 1 if side else chips - 1
            arrived(side, away, 0)
            (to_west(1, 1) if side else to_east(0, chips - 1)).start()
            to_mate(side, away).start()
        return do

    def back(side, away):
        def do():
            arrived(side, away, 0)
            to_mate(side, away).start()
        return do

    for side in (0, 1):
        if_side(side, own_rows(side))
    for side in (0, 1):
        if_side(side, onward(side))
    for side in (0, 1):
        if_side(side, back(side, chips - 1 if side else 1))
    for side in (0, 1):
        if_side(side, back(side, 2))

    def rest(side):
        def do():
            to_east(side, 0).wait_send()
            to_west(side, 0).wait_send()
            (to_west(1, 1) if side else to_east(0, chips - 1)).wait_send()
            for away in range(chips):
                to_mate(side, away).wait_send()
        return do

    def from_mate(side):
        def do():
            for away in range(chips):
                arrived(side, away, 1)
        return do

    for side in (0, 1):
        if_side(side, from_mate(side))
    load.wait()
    unroll = 4

    def step(q, carry):
        parts = []
        for i in range(unroll):
            r = q * unroll + i
            at = [jnp.clip(cols[k, r] - (leaf * depth - HB), 0, depth + 2 * HB - 1) for k in range(NB)]
            far = jnp.concatenate([win[j] for j in at], axis=1)
            close = jnp.concatenate([home[j] for j in at], axis=1)
            blocks = jnp.concatenate([A[r, k] for k in range(NB)], axis=1)
            parts.append(dot_nt_fast(jnp.concatenate([far, close], axis=0), blocks))
        pair = jnp.concatenate([p[:-count] for p in parts], axis=1)
        here = pl.ds(pl.multiple_of(q * (unroll * 128), unroll * 128), unroll * 128)
        z[:, here] = pair
        near[:, here] = jnp.concatenate([p[-count:] for p in parts], axis=1)
        high, mid, low = split3(pair)
        tops = dot_nt_fast(high, jnp.concatenate([high, mid, low], axis=0))
        acc[0] += tops[:, :256] + dot_nt_fast(mid, mid)
        acc[1] += tops[:, 256:512] + tops[:, 512:]
        return carry

    acc[...] = jnp.zeros_like(acc)
    lax.fori_loop(0, depth // unroll, step, 0)
    store = pltpu.make_async_copy(z, z_out, z_sem)
    store.start()
    g = acc[0] + (acc[1] + jnp.transpose(acc[1]))
    gram[0] = g[:128, :128]
    gram[1] = g[:128, 128:]
    gram[2] = g[128:, 128:]

    slab = 128 // group
    rows_here = pl.ds(pl.multiple_of(me * slab, slab), slab)
    for j in range(3):
        part[0, j * slab:(j + 1) * slab, :] = gram[j, rows_here, :]

    def trade(h):
        return pltpu.make_async_remote_copy(
            src_ref=part.at[h], dst_ref=got.at[h], send_sem=pair_send.at[h], recv_sem=pair_recv.at[h],
            device_id=(partners[h], me), device_id_type=MESH,
        )

    def share(h, sample_from, sample_to, hop):
        return pltpu.make_async_remote_copy(
            src_ref=part.at[h + 1], dst_ref=levels.at[h, sample_from],
            send_sem=all_send.at[h, hop], recv_sem=all_recv.at[h, sample_from],
            device_id=(leaf, sample_to), device_id_type=MESH,
        )

    trade(0).start()
    for h in range(LEVELS):
        trade(h).wait_recv()
        total = part[h] + got[h]
        part[h + 1] = total
        if h + 1 < LEVELS:
            trade(h + 1).start()
        for hop in HOPS[:-1]:
            share(h, me, lax.rem(me + hop, group), hop).start()
        levels[h, me] = total
    for h in range(LEVELS):
        for hop in HOPS[:-1]:
            share(h, lax.rem(me + hop, group), me, hop).wait_recv()
    for h in range(LEVELS):
        trade(h).wait_send()
        for hop in HOPS[:-1]:
            share(h, me, lax.rem(me + hop, group), hop).wait_send()
    for side in (0, 1):
        if_side(side, rest(side))
    @pl.when(leaf < leaves - 1)
    def _():
        halo(0).wait_send()
    @pl.when(leaf > 0)
    def _():
        halo(1).wait_send()
    store.wait()


def gather(leaves, stiffness_block_row, stored_block_column, samples_t):
    f32 = jnp.float32
    count, width = samples_t.shape
    depth = width // 128
    group = 8
    order = group * count
    slab = 128 // group
    vmem = pl.BlockSpec(memory_space=pltpu.VMEM)
    far = pl.BlockSpec(memory_space=pl.ANY)
    dma = pltpu.SemaphoreType.DMA
    return pl.pallas_call(
        functools.partial(gather_kernel, leaves),
        out_shape=[
            jax.ShapeDtypeStruct((order, width), f32),
            jax.ShapeDtypeStruct((count, width), f32),
            jax.ShapeDtypeStruct((3, 128, 128), f32),
            jax.ShapeDtypeStruct((LEVELS, group, 3 * slab, 128), f32),
        ],
        in_specs=[pl.BlockSpec(memory_space=pltpu.SMEM), far, vmem],
        out_specs=[far, vmem, vmem, vmem],
        scratch_shapes=[
            pltpu.VMEM(stiffness_block_row.shape, stiffness_block_row.dtype),
            pltpu.VMEM((order, width), f32),
            pltpu.VMEM((2 * HB + depth, order, 128), samples_t.dtype),
            pltpu.VMEM((2 * HB + depth, count, 128), samples_t.dtype),
            pltpu.VMEM((2, order, order), f32),
            pltpu.VMEM((LEVELS + 1, 3 * slab, 128), f32),
            pltpu.VMEM((LEVELS, 3 * slab, 128), f32),
            dma,
            dma,
            dma((2,)),
            dma((2, 2)),
            dma((2, 2)),
            dma((2, group // 2)),
            dma((2, group // 2, 2)),
            dma((LEVELS,)),
            dma((LEVELS,)),
            dma((LEVELS, group)),
            dma((LEVELS, group)),
        ],
        compiler_params=pltpu.CompilerParams(collective_id=0, has_side_effects=True),
    )(jnp.transpose(stored_block_column), stiffness_block_row, samples_t)


def finish_kernel(g0, lv, near, z_far, products, bases, one, two, three, top, U, W, X, Y, z, z_sem):
    count, width = bases.shape
    load = pltpu.make_async_copy(z_far, z, z_sem)
    load.start()
    slab = lv.shape[2] // 3
    def block(b, j):
        if b == 0:
            return g0[j]
        return jnp.concatenate([lv[b - 1, s, j * slab:(j + 1) * slab, :] for s in range(lv.shape[1])], axis=0)
    cholesky_inverse(block, U, W, X, Y, 4)
    mine = pl.ds(pl.multiple_of(lax.axis_index("samp") * count, count), count)
    load.wait()
    products[...] = near[...] + z[mine, :]
    bases[...] = dot_nn(W[0, mine, :], z[...]) * math.sqrt(width)
    for k, out in enumerate((one, two, three)):
        out[...] = dot_nt(U[k, mine, :], W[k + 1])
    top[...] = U[3, mine, :] * (1.0 / math.sqrt(2**LEVELS * width))


def finish(gram, levels, near, z):
    order, width = z.shape
    count = near.shape[0]
    f32 = jnp.float32
    vmem = pl.BlockSpec(memory_space=pltpu.VMEM)
    return pl.pallas_call(
        finish_kernel,
        out_shape=[jax.ShapeDtypeStruct((count, width), f32)] * 2 + [jax.ShapeDtypeStruct((count, order), f32)] * 4,
        in_specs=[vmem, vmem, vmem, pl.BlockSpec(memory_space=pl.ANY)],
        out_specs=[vmem] * 6,
        scratch_shapes=[pltpu.VMEM((4, order, order), f32)] * 2 + [pltpu.VMEM((8 * RS, 128), f32)] * 2 + [pltpu.VMEM((order, width), f32), pltpu.SemaphoreType.DMA],
        cost_estimate=pl.CostEstimate(flops=10**10, bytes_accessed=4 << 20, transcendentals=0),
    )(gram, levels, near, z)


def shards(leaves, stiffness_block_row, stored_block_column, samples_t):
    z, near, gram, levels = gather(leaves, stiffness_block_row, stored_block_column, samples_t)
    products, bases, *transposed = finish(gram, levels, near, z)
    return (products, bases) + tuple(jnp.transpose(t) for t in transposed)


def solution(mesh):
    return jax.shard_map(
        functools.partial(shards, mesh.shape["leaf"]),
        mesh=mesh,
        in_specs=(P("leaf", None, None, None), P("leaf", None), P("samp", "leaf")),
        out_specs=(
            P("samp", "leaf"),
            P("samp", "leaf"),
            P("leaf", "samp"),
            P("leaf", "samp"),
            P("leaf", "samp"),
            P("leaf", "samp"),
        ),
        check_vma=False,
    )
```

```python
import functools, math
import jax, jax.numpy as jnp
from jax import lax
from jax.experimental import pallas as pl
from jax.experimental.pallas import tpu as pltpu

from jax.sharding import PartitionSpec as P

HB = 4
NB = 8
LEVELS = 3
HOPS = (4, 5, 3, 6, 2, 7, 1, 0)
MESH = pl.DeviceIdType.MESH
RS = 136

def split3(x):
    high = x.astype(jnp.bfloat16)
    rest = x - high.astype(jnp.float32)
    mid = rest.astype(jnp.bfloat16)
    low = (rest - mid.astype(jnp.float32)).astype(jnp.bfloat16)
    return high, mid, low


def dot_split(a, b, over_a, over_b):
    free = 1 - over_a
    count = a.shape[free]
    parts = split3(a)
    out = None
    for k in (2, 1, 0):
        left = parts[0] if k == 2 else jnp.concatenate(parts[:3 - k], axis=free)
        piece = lax.dot_general(left, b[k], (((over_a,), (over_b,)), ((), ())), preferred_element_type=jnp.float32)
        for i in reversed(range(3 - k)):
            term = piece[i * count:(i + 1) * count]
            out = term if out is None else out + term
    return out


def dot_tn(a, b):
    return dot_split(a, split3(b), 0, 0)


def dot_nt(a, b):
    return dot_split(a, split3(b), 1, 1)


def dot_nt_fast(a, b):
    return lax.dot_general(a, b, (((1,), (1,)), ((), ())), preferred_element_type=jnp.float32)

def lane(v, j):
    return jnp.broadcast_to(v[:, j:j + 1], v.shape)

def rows(i):
    return pl.ds(i, 8, stride=RS)

def diagonal(xs, base, lo):
    return [[lane(xs[lo + p], base + lo + q) if q >= p else None for q in range(8)] for p in range(8)]

def factor(X, Y, nb, sp=16):
    column = lax.broadcasted_iota(jnp.int32, (1, 128), 1)
    for t in range(128 // sp):
        base = t * sp
        if t:
            solved = column < base
            for b in range(nb):
                lhs = X[b * RS:b * RS + base, base:base + sp]
                left = jnp.where(solved, Y[(4 + b) * RS:(4 + b) * RS + base, :], X[b * RS:b * RS + base, :])
                up = dot_tn(lhs, jnp.concatenate([left, Y[b * RS:b * RS + base, :]], axis=1))
                now = X[b * RS + base:b * RS + base + sp, :] - up[:, :128]
                X[b * RS + base:b * RS + base + sp, :] = now
                X[(4 + b) * RS + base:(4 + b) * RS + base + sp, :] = now
                Y[b * RS + base:b * RS + base + sp, :] -= up[:, 128:]
                Y[(4 + b) * RS + base:(4 + b) * RS + base + sp, :] -= jnp.where(solved, up[:, :128], 0.0)
        xs = [X[rows(base + i), :] for i in range(sp)]
        ys = [Y[rows(base + i), :] for i in range(sp)]
        a = diagonal(xs, base, 0)
        for lo in range(0, sp, 8):
            ahead = diagonal(xs, base, lo + 8) if lo + 8 < sp else None
            for p in range(8):
                r = lax.rsqrt(a[p][p])
                inv = r * r
                x = xs[lo + p] * r
                y = ys[lo + p] * r
                xs[lo + p], ys[lo + p] = x, y
                X[rows(base + lo + p), :] = x
                Y[rows(base + lo + p), :] = y
                for s in range(p + 1, 8):
                    u = a[p][s] * r
                    xs[lo + s] = xs[lo + s] - u * x
                    ys[lo + s] = ys[lo + s] - u * y
                    for q in range(s, 8):
                        a[s][q] = a[s][q] - (a[p][s] * a[p][q]) * inv
                if ahead is not None:
                    m = [lane(x, base + lo + 8 + j) for j in range(8)]
                    for s in range(8):
                        for q in range(s, 8):
                            ahead[s][q] = ahead[s][q] - m[s] * m[q]
                        xs[lo + 8 + s] = xs[lo + 8 + s] - m[s] * x
                        ys[lo + 8 + s] = ys[lo + 8 + s] - m[s] * y
            for i in range(lo + 16, sp):
                for p in range(8):
                    m = lane(xs[lo + p], base + i)
                    xs[i] = xs[i] - m * xs[lo + p]
                    ys[i] = ys[i] - m * ys[lo + p]
            a = ahead

def cholesky_inverse(G, U, W, X, Y, nb):
    r = lax.broadcasted_iota(jnp.int32, (128, 128), 0)
    c = lax.broadcasted_iota(jnp.int32, (128, 128), 1)
    eye = (r == c).astype(jnp.float32)
    up = c >= r
    zero = jnp.zeros((128, 128), jnp.float32)
    at = lambda g: slice(g * RS, g * RS + 128)
    for b in range(nb):
        X[at(b), :] = G(b, 0)
        X[at(4 + b), :] = G(b, 0)
        Y[at(b), :] = G(b, 1)
        Y[at(4 + b), :] = eye
    factor(X, Y, nb)
    for b in range(nb):
        u12 = Y[at(b), :]
        w11 = Y[at(4 + b), :]
        U[b, :128, :128] = jnp.where(up, X[at(b), :], zero)
        U[b, :128, 128:] = u12
        U[b, 128:, :128] = zero
        W[b, :128, :128] = w11
        W[b, :128, 128:] = zero
        z = dot_tn(u12, jnp.concatenate([u12, w11], axis=1))
        s = G(b, 2) - z[:, :128]
        X[at(b), :] = s
        X[at(4 + b), :] = s
        Y[at(b), :] = -z[:, 128:]
        Y[at(4 + b), :] = eye
    factor(X, Y, nb)
    for b in range(nb):
        U[b, 128:, 128:] = jnp.where(up, X[at(b), :], zero)
        W[b, 128:, :128] = Y[at(b), :]
        W[b, 128:, 128:] = Y[at(4 + b), :]

def greet(barrier, there, sample):
    pl.semaphore_signal(barrier, inc=1, device_id=(there, sample), device_id_type=MESH)


def gather_kernel(leaves, cols, stiff, own, z, near, gram, levels,
                  A, win, home, acc, part, got, load_sem,
                  halo_send, east_send, west_send, mate_send, recv, pair_send, pair_recv, all_send, all_recv):
    load = pltpu.make_async_copy(stiff, A, load_sem)
    load.start()
    leaf = lax.axis_index("leaf")
    me = lax.axis_index("samp")
    group = lax.axis_size("samp")
    chips = group // 2
    chip, core = me // 2, lax.rem(me, 2)
    count = own.shape[0]
    width = HB * 128
    east = 2 * lax.rem(chip + 1, chips) + core
    west = 2 * lax.rem(chip + chips - 1, chips) + core
    mate = 2 * chip + 1 - core
    barrier = pltpu.get_barrier_semaphore()
    @pl.when(leaf > 0)
    def _():
        greet(barrier, leaf - 1, me)
    @pl.when(leaf < leaves - 1)
    def _():
        greet(barrier, leaf + 1, me)
    for hop in HOPS[:-1]:
        greet(barrier, leaf, lax.rem(me + hop, group))
    partners = [leaf + (1 << h) - 2 * (1 << h) * lax.rem(leaf // (1 << h), 2) for h in range(LEVELS)]
    for h in range(1, LEVELS):
        greet(barrier, partners[h], me)
    depth = own.shape[1] // 128
    win[HB:HB + depth] = jnp.zeros((depth,) + win.shape[1:], win.dtype)
    for edge in (0, HB + depth):
        home[edge:edge + HB] = jnp.zeros((HB,) + home.shape[1:], home.dtype)
    for j in range(depth):
        home[HB + j] = own[:, j * 128:(j + 1) * 128]
    @pl.when(leaf == 0)
    def _():
        win[:HB] = jnp.zeros((HB,) + win.shape[1:], win.dtype)
    @pl.when(leaf == leaves - 1)
    def _():
        win[HB + depth:] = jnp.zeros((HB,) + win.shape[1:], win.dtype)
    neighbours = jnp.minimum(leaf, 1) + jnp.minimum(leaves - 1 - leaf, 1)
    pl.semaphore_wait(barrier, group - 1 + LEVELS - 1 + neighbours)

    def place(side, sample):
        return win.at[pl.ds(side * (HB + depth), HB), pl.ds(pl.multiple_of(sample * count, count), count), :]

    def send(source, side, sample, send_sem, slot, there, to):
        return pltpu.make_async_remote_copy(
            src_ref=source, dst_ref=place(side, sample), send_sem=send_sem, recv_sem=recv.at[side, slot[0], slot[1]],
            device_id=(there, to), device_id_type=MESH,
        )

    def halo(side):
        first = HB + (depth - HB) * (1 - side)
        return send(home.at[pl.ds(first, HB)], side, me, halo_send.at[side], (0, 0), leaf + 1 - 2 * side, me)

    def origin(away):
        return 2 * lax.rem(chip + away, chips) + core

    def to_east(side, away):
        return send(place(side, origin(away)), side, origin(away), east_send.at[side, away // 3],
                    ((away + chips - 1) % chips, 0), leaf, east)

    def to_west(side, away):
        return send(place(side, origin(away)), side, origin(away), west_send.at[side, away],
                    (away + 1, 0), leaf, west)

    def to_mate(side, away):
        return send(place(side, origin(away)), side, origin(away), mate_send.at[side, away], (away, 1), leaf, mate)

    def arrived(side, away, other):
        sample = 2 * lax.rem(chip + away, chips) + (1 - core if other else core)
        send(place(side, sample), side, sample, mate_send.at[side, away], (away, other), leaf, mate).wait_recv()

    def if_side(side, do):
        @pl.when((leaf < leaves - 1) if side else (leaf > 0))
        def _():
            do()

    @pl.when(leaf < leaves - 1)
    def _():
        halo(0).start()
    @pl.when(leaf > 0)
    def _():
        halo(1).start()

    def own_rows(side):
        def do():
            arrived(side, 0, 0)
            to_east(side, 0).start()
            to_west(side, 0).start()
            to_mate(side, 0).start()
        return do

    def onward(side):
        def do():
            away = 1 if side else chips - 1
            arrived(side, away, 0)
            (to_west(1, 1) if side else to_east(0, chips - 1)).start()
            to_mate(side, away).start()
        return do

    def back(side, away):
        def do():
            arrived(side, away, 0)
            to_mate(side, away).start()
        return do

    for side in (0, 1):
        if_side(side, own_rows(side))
    for side in (0, 1):
        if_side(side, onward(side))
    for side in (0, 1):
        if_side(side, back(side, chips - 1 if side else 1))
    for side in (0, 1):
        if_side(side, back(side, 2))

    def rest(side):
        def do():
            to_east(side, 0).wait_send()
            to_west(side, 0).wait_send()
            (to_west(1, 1) if side else to_east(0, chips - 1)).wait_send()
            for away in range(chips):
                to_mate(side, away).wait_send()
        return do

    def from_mate(side):
        def do():
            for away in range(chips):
                arrived(side, away, 1)
        return do

    for side in (0, 1):
        if_side(side, from_mate(side))
    load.wait()
    unroll = 4

    def step(q, carry):
        parts = []
        for i in range(unroll):
            r = q * unroll + i
            at = [jnp.clip(cols[k, r] - (leaf * depth - HB), 0, depth + 2 * HB - 1) for k in range(NB)]
            far = jnp.concatenate([win[j] for j in at], axis=1)
            close = jnp.concatenate([home[j] for j in at], axis=1)
            blocks = jnp.concatenate([A[r, k] for k in range(NB)], axis=1)
            parts.append(dot_nt_fast(jnp.concatenate([far, close], axis=0), blocks))
        pair = jnp.concatenate([p[:-count] for p in parts], axis=1)
        here = pl.ds(pl.multiple_of(q * (unroll * 128), unroll * 128), unroll * 128)
        z[:, here] = pair
        near[:, here] = jnp.concatenate([p[-count:] for p in parts], axis=1)
        high, mid, low = split3(pair)
        tops = dot_nt_fast(high, jnp.concatenate([high, mid, low], axis=0))
        acc[0] += tops[:, :256] + dot_nt_fast(mid, mid)
        acc[1] += tops[:, 256:512] + tops[:, 512:]
        return carry

    acc[...] = jnp.zeros_like(acc)
    lax.fori_loop(0, depth // unroll, step, 0)
    g = acc[0] + (acc[1] + jnp.transpose(acc[1]))
    gram[0] = g[:128, :128]
    gram[1] = g[:128, 128:]
    gram[2] = g[128:, 128:]

    slab = 128 // group
    rows_here = pl.ds(pl.multiple_of(me * slab, slab), slab)
    for j in range(3):
        part[0, j * slab:(j + 1) * slab, :] = gram[j, rows_here, :]

    def trade(h):
        return pltpu.make_async_remote_copy(
            src_ref=part.at[h], dst_ref=got.at[h], send_sem=pair_send.at[h], recv_sem=pair_recv.at[h],
            device_id=(partners[h], me), device_id_type=MESH,
        )

    def share(h, sample_from, sample_to, hop):
        return pltpu.make_async_remote_copy(
            src_ref=part.at[h + 1], dst_ref=levels.at[h, sample_from],
            send_sem=all_send.at[h, hop], recv_sem=all_recv.at[h, sample_from],
            device_id=(leaf, sample_to), device_id_type=MESH,
        )

    trade(0).start()
    for h in range(LEVELS):
        trade(h).wait_recv()
        total = part[h] + got[h]
        part[h + 1] = total
        if h + 1 < LEVELS:
            trade(h + 1).start()
        for hop in HOPS[:-1]:
            share(h, me, lax.rem(me + hop, group), hop).start()
        levels[h, me] = total
    for h in range(LEVELS):
        for hop in HOPS[:-1]:
            share(h, lax.rem(me + hop, group), me, hop).wait_recv()
    for h in range(LEVELS):
        trade(h).wait_send()
        for hop in HOPS[:-1]:
            share(h, me, lax.rem(me + hop, group), hop).wait_send()
    for side in (0, 1):
        if_side(side, rest(side))
    @pl.when(leaf < leaves - 1)
    def _():
        halo(0).wait_send()
    @pl.when(leaf > 0)
    def _():
        halo(1).wait_send()


def gather(leaves, stiffness_block_row, stored_block_column, samples_t):
    f32 = jnp.float32
    count, width = samples_t.shape
    depth = width // 128
    group = 8
    order = group * count
    slab = 128 // group
    vmem = pl.BlockSpec(memory_space=pltpu.VMEM)
    dma = pltpu.SemaphoreType.DMA
    return pl.pallas_call(
        functools.partial(gather_kernel, leaves),
        out_shape=[
            jax.ShapeDtypeStruct((order, width), f32),
            jax.ShapeDtypeStruct((count, width), f32),
            jax.ShapeDtypeStruct((3, 128, 128), f32),
            jax.ShapeDtypeStruct((LEVELS, group, 3 * slab, 128), f32),
        ],
        in_specs=[pl.BlockSpec(memory_space=pltpu.SMEM), pl.BlockSpec(memory_space=pltpu.HBM), vmem],
        out_specs=[vmem] * 4,
        scratch_shapes=[
            pltpu.VMEM(stiffness_block_row.shape, stiffness_block_row.dtype),
            pltpu.VMEM((2 * HB + depth, order, 128), samples_t.dtype),
            pltpu.VMEM((2 * HB + depth, count, 128), samples_t.dtype),
            pltpu.VMEM((2, order, order), f32),
            pltpu.VMEM((LEVELS + 1, 3 * slab, 128), f32),
            pltpu.VMEM((LEVELS, 3 * slab, 128), f32),
            dma,
            dma((2,)),
            dma((2, 2)),
            dma((2, 2)),
            dma((2, group // 2)),
            dma((2, group // 2, 2)),
            dma((LEVELS,)),
            dma((LEVELS,)),
            dma((LEVELS, group)),
            dma((LEVELS, group)),
        ],
        compiler_params=pltpu.CompilerParams(collective_id=0, has_side_effects=True, vmem_limit_bytes=52000000),
    )(jnp.transpose(stored_block_column), stiffness_block_row, samples_t)


def finish_kernel(g0, lv, near, z, products, bases, one, two, three, top, U, W, X, Y):
    count, width = bases.shape
    slab = lv.shape[2] // 3
    def block(b, j):
        if b == 0:
            return g0[j]
        return jnp.concatenate([lv[b - 1, s, j * slab:(j + 1) * slab, :] for s in range(lv.shape[1])], axis=0)
    cholesky_inverse(block, U, W, X, Y, 4)
    mine = pl.ds(pl.multiple_of(lax.axis_index("samp") * count, count), count)
    products[...] = near[...] + z[mine, :]
    bases[...] = dot_split(W[0, mine, :], split3(z[...]), 1, 0) * math.sqrt(width)
    for k, out in enumerate((one, two, three)):
        out[...] = dot_nt(U[k, mine, :], W[k + 1])
    top[...] = U[3, mine, :] * (1.0 / math.sqrt(2**LEVELS * width))


def finish(gram, levels, near, z):
    order, width = z.shape
    count = near.shape[0]
    f32 = jnp.float32
    vmem = pl.BlockSpec(memory_space=pltpu.VMEM)
    return pl.pallas_call(
        finish_kernel,
        out_shape=[jax.ShapeDtypeStruct((count, width), f32)] * 2 + [jax.ShapeDtypeStruct((count, order), f32)] * 4,
        in_specs=[vmem] * 4,
        out_specs=[vmem] * 6,
        scratch_shapes=[pltpu.VMEM((4, order, order), f32)] * 2 + [pltpu.VMEM((8 * RS, 128), f32)] * 2,
        compiler_params=pltpu.CompilerParams(vmem_limit_bytes=52000000),
        cost_estimate=pl.CostEstimate(flops=10**10, bytes_accessed=4 << 20, transcendentals=0),
    )(gram, levels, near, z)


def shards(leaves, stiffness_block_row, stored_block_column, samples_t):
    z, near, gram, levels = gather(leaves, stiffness_block_row, stored_block_column, samples_t)
    products, bases, *transposed = finish(gram, levels, near, z)
    return (products, bases) + tuple(jnp.transpose(t) for t in transposed)


def solution(mesh):
    return jax.shard_map(
        functools.partial(shards, mesh.shape["leaf"]),
        mesh=mesh,
        in_specs=(P("leaf", None, None, None), P("leaf", None), P("samp", "leaf")),
        out_specs=(
            P("samp", "leaf"),
            P("samp", "leaf"),
            P("leaf", "samp"),
            P("leaf", "samp"),
            P("leaf", "samp"),
            P("leaf", "samp"),
        ),
        check_vma=False,
    )
```

```python
import functools, math
import jax, jax.numpy as jnp
from jax import lax
from jax.experimental import pallas as pl
from jax.experimental.pallas import tpu as pltpu

from jax.sharding import PartitionSpec as P

HB = 4
NB = 8
LEVELS = 3
HOPS = (4, 5, 3, 6, 2, 7, 1, 0)
MESH = pl.DeviceIdType.MESH
RS = 136

def split3(x):
    high = x.astype(jnp.bfloat16)
    rest = x - high.astype(jnp.float32)
    mid = rest.astype(jnp.bfloat16)
    low = (rest - mid.astype(jnp.float32)).astype(jnp.bfloat16)
    return high, mid, low


def dot_split(a, b, over_a, over_b):
    free = 1 - over_a
    count = a.shape[free]
    parts = split3(a)
    out = None
    for k in (2, 1, 0):
        left = parts[0] if k == 2 else jnp.concatenate(parts[:3 - k], axis=free)
        piece = lax.dot_general(left, b[k], (((over_a,), (over_b,)), ((), ())), preferred_element_type=jnp.float32)
        for i in reversed(range(3 - k)):
            term = piece[i * count:(i + 1) * count]
            out = term if out is None else out + term
    return out


def dot_tn(a, b):
    return dot_split(a, split3(b), 0, 0)


def dot_nt(a, b):
    return dot_split(a, split3(b), 1, 1)


def dot_nt_fast(a, b):
    return lax.dot_general(a, b, (((1,), (1,)), ((), ())), preferred_element_type=jnp.float32)

def lane(v, j):
    return jnp.broadcast_to(v[:, j:j + 1], v.shape)

def rows(i):
    return pl.ds(i, 8, stride=RS)

def diagonal(xs, base, lo):
    return [[lane(xs[lo + p], base + lo + q) if q >= p else None for q in range(8)] for p in range(8)]

def factor(X, Y, nb, sp=16):
    column = lax.broadcasted_iota(jnp.int32, (1, 128), 1)
    for t in range(128 // sp):
        base = t * sp
        if t:
            solved = column < base
            for b in range(nb):
                lhs = X[b * RS:b * RS + base, base:base + sp]
                left = jnp.where(solved, Y[(4 + b) * RS:(4 + b) * RS + base, :], X[b * RS:b * RS + base, :])
                up = dot_tn(lhs, jnp.concatenate([left, Y[b * RS:b * RS + base, :]], axis=1))
                now = X[b * RS + base:b * RS + base + sp, :] - up[:, :128]
                X[b * RS + base:b * RS + base + sp, :] = now
                X[(4 + b) * RS + base:(4 + b) * RS + base + sp, :] = now
                Y[b * RS + base:b * RS + base + sp, :] -= up[:, 128:]
                Y[(4 + b) * RS + base:(4 + b) * RS + base + sp, :] -= jnp.where(solved, up[:, :128], 0.0)
        xs = [X[rows(base + i), :] for i in range(sp)]
        ys = [Y[rows(base + i), :] for i in range(sp)]
        a = diagonal(xs, base, 0)
        for lo in range(0, sp, 8):
            ahead = diagonal(xs, base, lo + 8) if lo + 8 < sp else None
            for p in range(8):
                r = lax.rsqrt(a[p][p])
                inv = r * r
                x = xs[lo + p] * r
                y = ys[lo + p] * r
                xs[lo + p], ys[lo + p] = x, y
                X[rows(base + lo + p), :] = x
                Y[rows(base + lo + p), :] = y
                for s in range(p + 1, 8):
                    u = a[p][s] * r
                    xs[lo + s] = xs[lo + s] - u * x
                    ys[lo + s] = ys[lo + s] - u * y
                    for q in range(s, 8):
                        a[s][q] = a[s][q] - (a[p][s] * a[p][q]) * inv
                if ahead is not None:
                    m = [lane(x, base + lo + 8 + j) for j in range(8)]
                    for s in range(8):
                        for q in range(s, 8):
                            ahead[s][q] = ahead[s][q] - m[s] * m[q]
                        xs[lo + 8 + s] = xs[lo + 8 + s] - m[s] * x
                        ys[lo + 8 + s] = ys[lo + 8 + s] - m[s] * y
            for i in range(lo + 16, sp):
                for p in range(8):
                    m = lane(xs[lo + p], base + i)
                    xs[i] = xs[i] - m * xs[lo + p]
                    ys[i] = ys[i] - m * ys[lo + p]
            a = ahead

def cholesky_inverse(G, U, W, X, Y, nb):
    r = lax.broadcasted_iota(jnp.int32, (128, 128), 0)
    c = lax.broadcasted_iota(jnp.int32, (128, 128), 1)
    eye = (r == c).astype(jnp.float32)
    up = c >= r
    zero = jnp.zeros((128, 128), jnp.float32)
    at = lambda g: slice(g * RS, g * RS + 128)
    for b in range(nb):
        X[at(b), :] = G(b, 0)
        X[at(4 + b), :] = G(b, 0)
        Y[at(b), :] = G(b, 1)
        Y[at(4 + b), :] = eye
    factor(X, Y, nb)
    for b in range(nb):
        u12 = Y[at(b), :]
        w11 = Y[at(4 + b), :]
        U[b, :128, :128] = jnp.where(up, X[at(b), :], zero)
        U[b, :128, 128:] = u12
        U[b, 128:, :128] = zero
        W[b, :128, :128] = w11
        W[b, :128, 128:] = zero
        z = dot_tn(u12, jnp.concatenate([u12, w11], axis=1))
        s = G(b, 2) - z[:, :128]
        X[at(b), :] = s
        X[at(4 + b), :] = s
        Y[at(b), :] = -z[:, 128:]
        Y[at(4 + b), :] = eye
    factor(X, Y, nb)
    for b in range(nb):
        U[b, 128:, 128:] = jnp.where(up, X[at(b), :], zero)
        W[b, 128:, :128] = Y[at(b), :]
        W[b, 128:, 128:] = Y[at(4 + b), :]

def greet(barrier, there, sample):
    pl.semaphore_signal(barrier, inc=1, device_id=(there, sample), device_id_type=MESH)


def gather_kernel(leaves, cols, stiff, samples, z, near, gram, levels,
                  A, own, own_sem, win, home, acc, part, got, load_sem,
                  halo_send, east_send, west_send, mate_send, recv, pair_send, pair_recv, all_send, all_recv):
    fetch = pltpu.make_async_copy(samples, own, own_sem)
    fetch.start()
    load = pltpu.make_async_copy(stiff, A, load_sem)
    load.start()
    leaf = lax.axis_index("leaf")
    me = lax.axis_index("samp")
    group = lax.axis_size("samp")
    chips = group // 2
    chip, core = me // 2, lax.rem(me, 2)
    count = own.shape[0]
    width = HB * 128
    east = 2 * lax.rem(chip + 1, chips) + core
    west = 2 * lax.rem(chip + chips - 1, chips) + core
    mate = 2 * chip + 1 - core
    barrier = pltpu.get_barrier_semaphore()
    @pl.when(leaf > 0)
    def _():
        greet(barrier, leaf - 1, me)
    @pl.when(leaf < leaves - 1)
    def _():
        greet(barrier, leaf + 1, me)
    for hop in HOPS[:-1]:
        greet(barrier, leaf, lax.rem(me + hop, group))
    partners = [leaf + (1 << h) - 2 * (1 << h) * lax.rem(leaf // (1 << h), 2) for h in range(LEVELS)]
    for h in range(1, LEVELS):
        greet(barrier, partners[h], me)
    depth = own.shape[1] // 128
    win[HB:HB + depth] = jnp.zeros((depth,) + win.shape[1:], win.dtype)
    for edge in (0, HB + depth):
        home[edge:edge + HB] = jnp.zeros((HB,) + home.shape[1:], home.dtype)
    fetch.wait()
    for j in range(depth):
        home[HB + j] = own[:, j * 128:(j + 1) * 128]
    @pl.when(leaf == 0)
    def _():
        win[:HB] = jnp.zeros((HB,) + win.shape[1:], win.dtype)
    @pl.when(leaf == leaves - 1)
    def _():
        win[HB + depth:] = jnp.zeros((HB,) + win.shape[1:], win.dtype)
    neighbours = jnp.minimum(leaf, 1) + jnp.minimum(leaves - 1 - leaf, 1)
    pl.semaphore_wait(barrier, group - 1 + LEVELS - 1 + neighbours)

    def place(side, sample):
        return win.at[pl.ds(side * (HB + depth), HB), pl.ds(pl.multiple_of(sample * count, count), count), :]

    def send(source, side, sample, send_sem, slot, there, to):
        return pltpu.make_async_remote_copy(
            src_ref=source, dst_ref=place(side, sample), send_sem=send_sem, recv_sem=recv.at[side, slot[0], slot[1]],
            device_id=(there, to), device_id_type=MESH,
        )

    def halo(side):
        first = HB + (depth - HB) * (1 - side)
        return send(home.at[pl.ds(first, HB)], side, me, halo_send.at[side], (0, 0), leaf + 1 - 2 * side, me)

    def origin(away):
        return 2 * lax.rem(chip + away, chips) + core

    def to_east(side, away):
        return send(place(side, origin(away)), side, origin(away), east_send.at[side, away // 3],
                    ((away + chips - 1) % chips, 0), leaf, east)

    def to_west(side, away):
        return send(place(side, origin(away)), side, origin(away), west_send.at[side, away],
                    (away + 1, 0), leaf, west)

    def to_mate(side, away):
        return send(place(side, origin(away)), side, origin(away), mate_send.at[side, away], (away, 1), leaf, mate)

    def arrived(side, away, other):
        sample = 2 * lax.rem(chip + away, chips) + (1 - core if other else core)
        send(place(side, sample), side, sample, mate_send.at[side, away], (away, other), leaf, mate).wait_recv()

    def if_side(side, do):
        @pl.when((leaf < leaves - 1) if side else (leaf > 0))
        def _():
            do()

    @pl.when(leaf < leaves - 1)
    def _():
        halo(0).start()
    @pl.when(leaf > 0)
    def _():
        halo(1).start()

    def own_rows(side):
        def do():
            arrived(side, 0, 0)
            to_east(side, 0).start()
            to_west(side, 0).start()
            to_mate(side, 0).start()
        return do

    def onward(side):
        def do():
            away = 1 if side else chips - 1
            arrived(side, away, 0)
            (to_west(1, 1) if side else to_east(0, chips - 1)).start()
            to_mate(side, away).start()
        return do

    def back(side, away):
        def do():
            arrived(side, away, 0)
            to_mate(side, away).start()
        return do

    for side in (0, 1):
        if_side(side, own_rows(side))
    for side in (0, 1):
        if_side(side, onward(side))
    for side in (0, 1):
        if_side(side, back(side, chips - 1 if side else 1))
    for side in (0, 1):
        if_side(side, back(side, 2))

    def rest(side):
        def do():
            to_east(side, 0).wait_send()
            to_west(side, 0).wait_send()
            (to_west(1, 1) if side else to_east(0, chips - 1)).wait_send()
            for away in range(chips):
                to_mate(side, away).wait_send()
        return do

    def from_mate(side):
        def do():
            for away in range(chips):
                arrived(side, away, 1)
        return do

    for side in (0, 1):
        if_side(side, from_mate(side))
    load.wait()
    unroll = 4

    def step(q, carry):
        parts = []
        for i in range(unroll):
            r = q * unroll + i
            at = [jnp.clip(cols[k, r] - (leaf * depth - HB), 0, depth + 2 * HB - 1) for k in range(NB)]
            far = jnp.concatenate([win[j] for j in at], axis=1)
            close = jnp.concatenate([home[j] for j in at], axis=1)
            blocks = jnp.concatenate([A[r, k] for k in range(NB)], axis=1)
            parts.append(dot_nt_fast(jnp.concatenate([far, close], axis=0), blocks))
        pair = jnp.concatenate([p[:-count] for p in parts], axis=1)
        here = pl.ds(pl.multiple_of(q * (unroll * 128), unroll * 128), unroll * 128)
        z[:, here] = pair
        near[:, here] = jnp.concatenate([p[-count:] for p in parts], axis=1)
        high, mid, low = split3(pair)
        tops = dot_nt_fast(high, jnp.concatenate([high, mid, low], axis=0))
        acc[0] += tops[:, :256] + dot_nt_fast(mid, mid)
        acc[1] += tops[:, 256:512] + tops[:, 512:]
        return carry

    acc[...] = jnp.zeros_like(acc)
    lax.fori_loop(0, depth // unroll, step, 0)
    g = acc[0] + (acc[1] + jnp.transpose(acc[1]))
    gram[0] = g[:128, :128]
    gram[1] = g[:128, 128:]
    gram[2] = g[128:, 128:]

    slab = 128 // group
    rows_here = pl.ds(pl.multiple_of(me * slab, slab), slab)
    for j in range(3):
        part[0, j * slab:(j + 1) * slab, :] = gram[j, rows_here, :]

    def trade(h):
        return pltpu.make_async_remote_copy(
            src_ref=part.at[h], dst_ref=got.at[h], send_sem=pair_send.at[h], recv_sem=pair_recv.at[h],
            device_id=(partners[h], me), device_id_type=MESH,
        )

    def share(h, sample_from, sample_to, hop):
        return pltpu.make_async_remote_copy(
            src_ref=part.at[h + 1], dst_ref=levels.at[h, sample_from],
            send_sem=all_send.at[h, hop], recv_sem=all_recv.at[h, sample_from],
            device_id=(leaf, sample_to), device_id_type=MESH,
        )

    trade(0).start()
    for h in range(LEVELS):
        trade(h).wait_recv()
        total = part[h] + got[h]
        part[h + 1] = total
        if h + 1 < LEVELS:
            trade(h + 1).start()
        for hop in HOPS[:-1]:
            share(h, me, lax.rem(me + hop, group), hop).start()
        levels[h, me] = total
    for h in range(LEVELS):
        for hop in HOPS[:-1]:
            share(h, lax.rem(me + hop, group), me, hop).wait_recv()
    for h in range(LEVELS):
        trade(h).wait_send()
        for hop in HOPS[:-1]:
            share(h, me, lax.rem(me + hop, group), hop).wait_send()
    for side in (0, 1):
        if_side(side, rest(side))
    @pl.when(leaf < leaves - 1)
    def _():
        halo(0).wait_send()
    @pl.when(leaf > 0)
    def _():
        halo(1).wait_send()


def gather(leaves, stiffness_block_row, stored_block_column, samples_t):
    f32 = jnp.float32
    count, width = samples_t.shape
    depth = width // 128
    group = 8
    order = group * count
    slab = 128 // group
    vmem = pl.BlockSpec(memory_space=pltpu.VMEM)
    dma = pltpu.SemaphoreType.DMA
    return pl.pallas_call(
        functools.partial(gather_kernel, leaves),
        out_shape=[
            jax.ShapeDtypeStruct((order, width), f32),
            jax.ShapeDtypeStruct((count, width), f32),
            jax.ShapeDtypeStruct((3, 128, 128), f32),
            jax.ShapeDtypeStruct((LEVELS, group, 3 * slab, 128), f32),
        ],
        in_specs=[pl.BlockSpec(memory_space=pltpu.SMEM), pl.BlockSpec(memory_space=pltpu.HBM), pl.BlockSpec(memory_space=pltpu.HBM)],
        out_specs=[vmem] * 4,
        scratch_shapes=[
            pltpu.VMEM(stiffness_block_row.shape, stiffness_block_row.dtype),
            pltpu.VMEM(samples_t.shape, samples_t.dtype),
            dma,
            pltpu.VMEM((2 * HB + depth, order, 128), samples_t.dtype),
            pltpu.VMEM((2 * HB + depth, count, 128), samples_t.dtype),
            pltpu.VMEM((2, order, order), f32),
            pltpu.VMEM((LEVELS + 1, 3 * slab, 128), f32),
            pltpu.VMEM((LEVELS, 3 * slab, 128), f32),
            dma,
            dma((2,)),
            dma((2, 2)),
            dma((2, 2)),
            dma((2, group // 2)),
            dma((2, group // 2, 2)),
            dma((LEVELS,)),
            dma((LEVELS,)),
            dma((LEVELS, group)),
            dma((LEVELS, group)),
        ],
        compiler_params=pltpu.CompilerParams(collective_id=0, has_side_effects=True, vmem_limit_bytes=52500000),
    )(jnp.transpose(stored_block_column), stiffness_block_row, pltpu.with_memory_space_constraint(samples_t, pltpu.HBM))


def finish_kernel(g0, lv, near, z, products, bases, one, two, three, top, U, W, X, Y):
    count, width = bases.shape
    slab = lv.shape[2] // 3
    def block(b, j):
        if b == 0:
            return g0[j]
        return jnp.concatenate([lv[b - 1, s, j * slab:(j + 1) * slab, :] for s in range(lv.shape[1])], axis=0)
    cholesky_inverse(block, U, W, X, Y, 4)
    mine = pl.ds(pl.multiple_of(lax.axis_index("samp") * count, count), count)
    products[...] = near[...] + z[mine, :]
    bases[...] = dot_split(W[0, mine, :], split3(z[...]), 1, 0) * math.sqrt(width)
    for k, out in enumerate((one, two, three)):
        out[...] = dot_nt(U[k, mine, :], W[k + 1])
    top[...] = U[3, mine, :] * (1.0 / math.sqrt(2**LEVELS * width))


def finish(gram, levels, near, z):
    order, width = z.shape
    count = near.shape[0]
    f32 = jnp.float32
    vmem = pl.BlockSpec(memory_space=pltpu.VMEM)
    return pl.pallas_call(
        finish_kernel,
        out_shape=[jax.ShapeDtypeStruct((count, width), f32)] * 2 + [jax.ShapeDtypeStruct((count, order), f32)] * 4,
        in_specs=[vmem] * 4,
        out_specs=[vmem] * 6,
        scratch_shapes=[pltpu.VMEM((4, order, order), f32)] * 2 + [pltpu.VMEM((8 * RS, 128), f32)] * 2,
        compiler_params=pltpu.CompilerParams(vmem_limit_bytes=52500000),
        cost_estimate=pl.CostEstimate(flops=10**10, bytes_accessed=4 << 20, transcendentals=0),
    )(gram, levels, near, z)


def shards(leaves, stiffness_block_row, stored_block_column, samples_t):
    z, near, gram, levels = gather(leaves, stiffness_block_row, stored_block_column, samples_t)
    products, bases, *transposed = finish(gram, levels, near, z)
    return (products, bases) + tuple(jnp.transpose(t) for t in transposed)


def solution(mesh):
    return jax.shard_map(
        functools.partial(shards, mesh.shape["leaf"]),
        mesh=mesh,
        in_specs=(P("leaf", None, None, None), P("leaf", None), P("samp", "leaf")),
        out_specs=(
            P("samp", "leaf"),
            P("samp", "leaf"),
            P("leaf", "samp"),
            P("leaf", "samp"),
            P("leaf", "samp"),
            P("leaf", "samp"),
        ),
        check_vma=False,
    )
```
